32 devices in a mesh: rows: 8 (over z, x), cols: 4 (over y, core).
Axes of the slice: x: 2, y: 2, z: 4, core: 2. Of those that a mesh axis runs over, the one named last changes fastest.
Arguments:
- image_in: bfloat16 [1, 128, 384, 256], P(None, 'rows', 'cols'), may hold values from -6 to 6
- cotangent: bfloat16 [1, 128, 384, 256], P(None, 'rows', 'cols'), may hold values from -6 to 6
- first_kernel: bfloat16 [3, 3, 256, 256], replicated, may hold values from -0.125 to 0.125
- first_bias: float32 [256], replicated, may hold values from -3 to 3
- second_kernel: bfloat16 [3, 3, 256, 256], replicated, may hold values from -0.125 to 0.125
- first_center: float32 [32], replicated, may hold values from -3 to 3
- first_inverse: float32 [32], replicated, may hold values from 0.5 to 2
- first_gain: float32 [256], replicated, may hold values from 0.5 to 1.5
- first_shift: float32 [256], replicated, may hold values from -3 to 3
- second_center: float32 [32], replicated, may hold values from -3 to 3
- second_inverse: float32 [32], replicated, may hold values from 0.5 to 2
- second_gain: float32 [256], replicated, may hold values from 0.5 to 1.5
- second_shift: float32 [256], replicated, may hold values from -3 to 3
Outputs:
- image_grad: bfloat16 [1, 128, 384, 256], P(None, 'rows', 'cols')
The draws below stay inside these ranges and needn't reach their ends.
All inputs are finite; a program needn't handle non-finite values.
Results may differ from the reference program's by a relative error of at most 0.0044.
Values may be sent and summed in bfloat16 or wider, within the bound.
A program may use at most 64 MiB of HBM per device.

```python
import math
import jax
import jax.numpy as jnp
from jax import lax

CHANNELS = 256
GROUPS = 32
IMAGES = 1
HEIGHT = 128
WIDTH = 384


def block_levels(key, shape, pieces, least, largest):
    loudness, own = 1.0, jax.random.fold_in(key, 6)
    for dim, shards_of in pieces:
        draws = jnp.exp(jax.random.uniform(jax.random.fold_in(own, dim), (shards_of,), jnp.float32, least / len(pieces), largest / len(pieces)))
        loudness = loudness * jnp.repeat(draws, shape[dim] // shards_of).reshape([-1 if axis == dim else 1 for axis in range(len(shape))])
    return loudness


def noise(stream_key, shape, spread, reach, cuts=(), kind=jnp.bfloat16):
    drawn = spread * jax.random.normal(stream_key, shape, jnp.float32)
    if cuts:
        drawn = drawn * block_levels(stream_key, shape, cuts, -0.22, 0.18)
    return jnp.clip(drawn, -reach, reach).astype(kind)


def setup_inputs(seed: int = 0) -> dict:
    seeds = jax.random.split(jax.random.key(seed), 14)
    return {
        "image_in": noise(seeds[0], (IMAGES, HEIGHT, WIDTH, CHANNELS), 1.0, 6.0, ((1, 8), (2, 4))),
        "cotangent": noise(seeds[1], (IMAGES, HEIGHT, WIDTH, CHANNELS), 1.0, 6.0, ((1, 8), (2, 4))),
        "first_kernel": noise(seeds[2], (3, 3, CHANNELS, CHANNELS), (9 * CHANNELS) ** -0.5, 0.125),
        "first_bias": noise(seeds[3], (CHANNELS,), 0.5, 3.0, (), jnp.float32),
        "second_kernel": noise(seeds[4], (3, 3, CHANNELS, CHANNELS), (9 * CHANNELS) ** -0.5, 0.125),
        "first_center": noise(seeds[5], (GROUPS,), 0.5, 3.0, (), jnp.float32),
        "first_inverse": jnp.clip(jnp.exp(jax.random.uniform(seeds[6], (GROUPS,), jnp.float32, math.log(0.5), math.log(2.0))), 0.5, 2.0),
        "first_gain": jnp.clip(1.0 + 0.1 * jax.random.normal(seeds[7], (CHANNELS,), jnp.float32), 0.5, 1.5),
        "first_shift": noise(seeds[8], (CHANNELS,), 0.5, 3.0, (), jnp.float32),
        "second_center": noise(seeds[9], (GROUPS,), 0.5, 3.0, (), jnp.float32),
        "second_inverse": jnp.clip(jnp.exp(jax.random.uniform(seeds[10], (GROUPS,), jnp.float32, math.log(0.5), math.log(2.0))), 0.5, 2.0),
        "second_gain": jnp.clip(1.0 + 0.1 * jax.random.normal(seeds[11], (CHANNELS,), jnp.float32), 0.5, 1.5),
        "second_shift": noise(seeds[12], (CHANNELS,), 0.5, 3.0, (), jnp.float32),
    }


def per_channel(stat):
    return jnp.repeat(stat, CHANNELS // GROUPS)


def silu_slope(value):
    sig = jax.nn.sigmoid(value)
    return sig * (1.0 + value * (1.0 - sig))


def convolve(field, kernel):
    return lax.conv_general_dilated(field.astype(jnp.float32), kernel.astype(jnp.float32), (1, 1), "SAME", dimension_numbers=("NHWC", "HWIO", "NHWC"), preferred_element_type=jnp.float32)


def flipped(kernel):
    return jnp.transpose(kernel[::-1, ::-1], (0, 1, 3, 2))


def reference(image_in, cotangent, first_kernel, first_bias, second_kernel, first_center, first_inverse, first_gain, first_shift, second_center, second_inverse, second_gain, second_shift):
    scale_one = per_channel(first_inverse) * first_gain
    scale_two = per_channel(second_inverse) * second_gain
    kernel_back_two = flipped(second_kernel)
    kernel_back_one = flipped(first_kernel)

    def one_image(pair):
        image, grad_out = pair
        image = image[None]
        grad_out = grad_out[None]
        pre_one = (image.astype(jnp.float32) - per_channel(first_center)) * scale_one + first_shift
        act_one = jax.nn.silu(pre_one).astype(jnp.bfloat16)
        pre_two = (convolve(act_one, first_kernel) + first_bias - per_channel(second_center)) * scale_two + second_shift
        back_two = convolve(grad_out, kernel_back_two)
        back_inner = (back_two * silu_slope(pre_two) * scale_two).astype(jnp.bfloat16)
        back_one = convolve(back_inner, kernel_back_one)
        result = grad_out.astype(jnp.float32) + back_one * silu_slope(pre_one) * scale_one
        return result.astype(jnp.bfloat16)[0]

    return lax.map(one_image, (image_in, cotangent))
```

```python
import functools

import jax
import jax.numpy as jnp
from jax import lax
from jax.experimental import pallas as pl
from jax.experimental.pallas import tpu as pltpu
from jax.sharding import PartitionSpec as P

MESH = pl.DeviceIdType.MESH
TILE = 16
LANES = 128
NEAR = 2
SIDES = (-1, 1)


def sigmoid(value):
    return 0.5 + 0.5 * jnp.tanh(0.5 * value)


def silu_slope(value):
    sig = sigmoid(value)
    return sig * (1.0 + value * (1.0 - sig))


def kernel(
    rows,
    cols,
    chans,
    groups,
    x_hbm,
    g_hbm,
    k1_hbm,
    b1_hbm,
    k2_hbm,
    c1_hbm,
    v1_hbm,
    n1_hbm,
    s1_hbm,
    c2_hbm,
    v2_hbm,
    n2_hbm,
    s2_hbm,
    o_ref,
    xg,
    k1,
    k2,
    k1t,
    k2t,
    vecs,
    scal,
    params,
    stage,
    ins,
    outs,
    gain,
    cat,
    side_cat,
    edge_cat,
    icat,
    back_main,
    back_side,
    pre_edge,
    side_edge,
    out_edge,
    row_halo,
    pack,
    col_halo,
    corner_f32,
    corner_out,
    corner_in,
    leave,
    enter,
    load_sem,
    row_send,
    row_recv,
    col_send,
    col_recv,
    corner_send,
    corner_recv,
    leave_send,
    enter_recv,
):
    span = cols + 2 * TILE
    step = cols // TILE
    lane_parts = [slice(k, k + LANES) for k in range(0, chans, LANES)]
    f32, bf16 = jnp.float32, jnp.bfloat16
    my_row, my_col = lax.axis_index("rows"), lax.axis_index("cols")
    n_rows, n_cols = lax.axis_size("rows"), lax.axis_size("cols")
    above, below = my_row > 0, my_row < n_rows - 1
    left, right = my_col > 0, my_col < n_cols - 1
    row_there, col_there = (above, below), (left, right)

    barrier = pltpu.get_barrier_semaphore()
    for n, side in enumerate(SIDES):

        @pl.when(col_there[n])
        def _():
            pl.semaphore_signal(
                barrier, inc=1, device_id=(my_row, my_col + side), device_id_type=MESH
            )

        @pl.when(row_there[n])
        def _():
            pl.semaphore_signal(
                barrier, inc=1, device_id=(my_row + side, my_col), device_id_type=MESH
            )

    load_k2 = pltpu.make_async_copy(k2_hbm, k2, load_sem.at[0])
    load_k1 = pltpu.make_async_copy(k1_hbm, k1, load_sem.at[1])
    load_x = pltpu.make_async_copy(x_hbm.at[0], xg.at[0], load_sem.at[2])
    load_g = pltpu.make_async_copy(g_hbm.at[0], xg.at[1], load_sem.at[3])
    for copy in (load_g, load_k2, load_x, load_k1):
        copy.start()
    for n, ref in enumerate((b1_hbm, n1_hbm, s1_hbm, n2_hbm, s2_hbm)):
        pltpu.make_async_copy(ref, vecs.at[n], load_sem.at[4]).start()
    for n, ref in enumerate((c1_hbm, v1_hbm, c2_hbm, v2_hbm)):
        pltpu.make_async_copy(ref, scal.at[n], load_sem.at[5 + n]).start()

    def one(there):
        return jnp.where(there, 1, 0)

    pl.semaphore_wait(barrier, one(above) + one(below) + one(left) + one(right))

    def row_copy(n, m):
        return pltpu.make_async_remote_copy(
            src_ref=(x_hbm, g_hbm)[m].at[0, (0, rows - 1)[n]],
            dst_ref=row_halo.at[1 - n, m],
            send_sem=row_send.at[n],
            recv_sem=row_recv.at[1 - n],
            device_id=(my_row + SIDES[n], my_col),
            device_id_type=MESH,
        )

    def row_both(n):
        return pltpu.make_async_remote_copy(
            src_ref=row_halo.at[1 - n],
            dst_ref=row_halo.at[1 - n],
            send_sem=row_send.at[n],
            recv_sem=row_recv.at[1 - n],
            device_id=(my_row + SIDES[n], my_col),
            device_id_type=MESH,
        )

    def col_copy(n, m):
        return pltpu.make_async_remote_copy(
            src_ref=pack.at[n, m],
            dst_ref=col_halo.at[1 - n, m],
            send_sem=col_send.at[n, m],
            recv_sem=col_recv.at[1 - n, m],
            device_id=(my_row, my_col + SIDES[n]),
            device_id_type=MESH,
        )

    def corner_copy(n):
        return pltpu.make_async_remote_copy(
            src_ref=corner_out.at[n],
            dst_ref=corner_in.at[1 - n],
            send_sem=corner_send.at[n],
            recv_sem=corner_recv.at[1 - n],
            device_id=(my_row + SIDES[n], my_col),
            device_id_type=MESH,
        )

    def onward(n):
        return pltpu.make_async_remote_copy(
            src_ref=leave.at[n],
            dst_ref=enter.at[1 - n],
            send_sem=leave_send.at[n],
            recv_sem=enter_recv.at[1 - n],
            device_id=(my_row + SIDES[n], my_col),
            device_id_type=MESH,
        )

    for n in range(2):

        @pl.when(row_there[n])
        def _():
            for m in (1, 0):
                row_copy(n, m).start()

    def flip(source, target):
        for i in range(3):
            for j in range(3):
                target[i, j] = source[2 - i, 2 - j].T

    def put(ref, at, value):
        for k, lanes in enumerate(lane_parts):
            ref[(*at[:-1], k, at[-1])] = value[:, lanes]

    def take(ref, at):
        return jnp.concatenate([ref[(*at[:-1], k, at[-1])] for k in range(len(lane_parts))], 1)

    def near(h, n):
        first = h * span + (TILE - NEAR, TILE + cols)[n]
        return slice(first, first + NEAR)

    def inside(h):
        return slice(h * span + TILE, h * span + TILE + cols)

    def down(h, col):
        return pl.ds(h * span + TILE + col, rows, stride=span)

    def tiles(m, h, which):
        for t in which:
            part = take(stage, (m, pl.ds(h * span + TILE + t - 1, TILE, stride=step)))
            cat[m, h, t * TILE : (t + 1) * TILE] = part.astype(bf16)

    def send_cols(m):
        for n in range(2):
            for c in range(NEAR):
                part = take(stage, (m, down(1, (0, cols - NEAR)[n] + c)))
                pack[n, m, c * rows : (c + 1) * rows] = part.astype(bf16)
        for n in range(2):

            @pl.when(col_there[n])
            def _():
                col_copy(n, m).start()

    for h in (0, rows + 1):
        for m in range(2):
            cat[m, h] = jnp.zeros(cat.shape[2:], bf16)
            for n in range(2):
                first = h * span + (TILE - 8, TILE + cols - 8)[n]
                put(stage, (m, slice(first, first + TILE)), jnp.zeros((TILE, chans), f32))
        icat[h] = jnp.zeros(icat.shape[1:], bf16)
    edge_cat[...] = jnp.zeros(edge_cat.shape, f32)

    load_g.wait()
    for n in range(rows):
        put(stage, (1, inside(n + 1)), xg[1, n].astype(f32))
    send_cols(1)
    pltpu.make_async_copy(vecs, vecs, load_sem.at[4]).wait()
    for n, ref in enumerate((c1_hbm, v1_hbm, c2_hbm, v2_hbm)):
        pltpu.make_async_copy(ref, scal.at[n], load_sem.at[5 + n]).wait()
    load_x.wait()
    load_k2.wait()
    lane_group = lax.broadcasted_iota(jnp.int32, (1, chans), 1) // (chans // groups)

    def spread(n):
        total = jnp.zeros((1, chans), f32)
        for q in range(groups):
            total = jnp.where(lane_group == q, scal[n, q], total)
        return total

    scale1 = spread(1) * vecs[1]
    scale2 = spread(3) * vecs[3]
    params[0] = scale1
    params[1] = vecs[2] - spread(0) * scale1
    params[2] = scale2
    params[3] = (vecs[0] - spread(2)) * scale2 + vecs[4]

    def activate(value):
        pre = value.astype(f32) * params[0] + params[1]
        return pre * sigmoid(pre)

    for n in range(rows):
        put(stage, (0, inside(n + 1)), activate(xg[0, n]))
    send_cols(0)

    every = (0, 1, 2)

    def contract(weights, taps, pieces):
        lhs = []
        for i in taps:
            for j in range(3):
                stack = [part for piece in pieces for part in piece(i, j)]
                lhs.append(stack[0] if len(stack) == 1 else jnp.concatenate(stack, 0))
        rhs = weights[taps[0] : taps[-1] + 1].reshape(len(taps) * 3 * chans, chans)
        return jnp.dot(jnp.concatenate(lhs, 1), rhs, preferred_element_type=f32)

    def body(ref, place, count, start, width):
        def piece(i, j):
            part = ref[place + i : place + i + count, (start + j) * TILE : (start + j) * TILE + width]
            return [part.reshape(count * width, chans)]

        return piece

    def beside(m, n):
        return lambda i, j: [side_cat[m, 3 * i + j, n * TILE : (n + 1) * TILE]]

    half = rows // 2
    halves = ((0, 0), (1, half))

    flip(k2, k2t)
    for h in range(1, rows + 1):
        tiles(1, h, range(1, step + 1))
    core = cols - 2 * TILE
    for q, place in halves:
        back = contract(k2t, every, [body(cat.at[1], place, half, 1, core)])
        for n in range(half):
            back_main[place + n, TILE : TILE + core] = back[n * core : (n + 1) * core]
    for n in range(rows):
        pre = xg[0, n].astype(f32) * params[0] + params[1]
        gain[n] = silu_slope(pre) * params[0]
        tiles(0, n + 1, range(1, step + 1))

    load_k1.wait()
    for m in (1, 0):
        for n in range(2):

            @pl.when(col_there[n])
            def _():
                col_copy(1 - n, m).wait_recv()

    for m in range(2):
        for n in range(2):
            for c in range(NEAR):
                part = col_halo[n, m, c * rows : (c + 1) * rows].astype(f32)
                part = jnp.where(col_there[n], part, 0.0)
                put(stage, (m, down(1, (-NEAR, cols)[n] + c)), part)
    for n, h in enumerate((1, rows)):
        for m in range(2):
            for q in range(2):
                first = (2 * m + q) * NEAR
                corner_f32[n, first : first + NEAR] = take(stage, (m, near(h, q)))
        corner_out[n] = corner_f32[n].astype(bf16)
    for n in range(2):

        @pl.when(row_there[n])
        def _():
            corner_copy(n).start()

    def side_tiles(m):
        for n, col in enumerate((-1, cols)):
            for i in range(3):
                for j in range(3):
                    part = take(stage, (m, down(i, col + j - 1)))
                    side_cat[m, 3 * i + j, n * TILE : n * TILE + rows] = part.astype(bf16)

    def inner_value(back, pre):
        return back * silu_slope(pre * params[2] + params[3]) * params[2]

    def inner_store(n, value):
        for t in range(step):
            at = pl.ds(n * span + TILE + t, TILE, stride=step)
            put(ins, (at,), value[t * TILE : (t + 1) * TILE])

    def inner_tiles(n, h):
        for t in range(step + 2):
            part = take(ins, (pl.ds(n * span + TILE + t - 1, TILE, stride=step),))
            icat[h, t * TILE : (t + 1) * TILE] = part.astype(bf16)

    for m in range(2):
        for h in range(1, rows + 1):
            tiles(m, h, (0, step + 1))
        side_tiles(m)
    for q, place in halves:
        outer = [body(cat.at[1], place, half, start, TILE) for start in (0, step - 1)]
        back = contract(k2t, every, [*outer, beside(1, q)])
        for n in range(half):
            back_main[place + n, :TILE] = back[n * TILE : (n + 1) * TILE]
            back_main[place + n, cols - TILE :] = back[(half + n) * TILE : (half + n + 1) * TILE]
        back_side[q * TILE : (q + 1) * TILE] = back[rows * TILE :]
    for q, place in halves:
        pre = contract(k1, every, [body(cat.at[0], place, half, 0, cols), beside(0, q)])
        for n in range(half):
            part = pre[n * cols : (n + 1) * cols]
            if place + n in (0, rows - 1):
                pre_edge[q] = part
            else:
                inner_store(place + n, inner_value(back_main[place + n], part))
        part, back = pre[half * cols :], back_side[q * TILE : (q + 1) * TILE]
        own = jnp.where(col_there[q], inner_value(back, part), 0.0)
        put(ins, (down(0, (-1, cols)[q]),), own)
        for n, r in enumerate((0, rows - 1)):
            side_edge[0, n, q : q + 1] = part[r : r + 1]
            side_edge[1, n, q : q + 1] = back[r : r + 1]
    flip(k1, k1t)
    for n in range(1, rows - 1):
        inner_tiles(n, n + 1)

    for n in range(2):

        @pl.when(row_there[n])
        def _():
            row_both(1 - n).wait_recv()
            corner_copy(1 - n).wait_recv()

    edges = ((0, 0, 0), (rows + 1, rows - 1, 2))
    for n, (h, place, tap) in enumerate(edges):
        there = row_there[n]
        value = jnp.where(there, activate(row_halo[n, 0]), 0.0)
        put(stage, (0, inside(h)), value)
        value = jnp.where(there, row_halo[n, 1].astype(f32), 0.0)
        put(stage, (1, inside(h)), value)
        corner_f32[n] = jnp.where(there, corner_in[n].astype(f32), 0.0)
        for m in range(2):
            for q in range(2):
                first = (2 * m + q) * NEAR
                put(stage, (m, near(h, q)), corner_f32[n, first : first + NEAR])
            tiles(m, h, range(step + 2))
            for j in range(3):
                for q, col in enumerate((-1, cols)):
                    at = h * span + TILE + col + j - 1
                    edge_cat[n, m, j, q : q + 1] = take(stage, (m, slice(at, at + 1)))

    def ends(n, m):
        return lambda i, j: [edge_cat[n, m, j].astype(bf16)]

    for n, (h, place, tap) in enumerate(edges):
        back = contract(k2t, (tap,), [body(cat.at[1], place, 1, 0, cols), ends(n, 1)])
        pre = contract(k1, (tap,), [body(cat.at[0], place, 1, 0, cols), ends(n, 0)])
        value = inner_value(back[:cols] + back_main[place], pre[:cols] + pre_edge[n])
        inner_store(place, value)
        value = inner_value(back[cols:] + side_edge[1, n], pre[cols:] + side_edge[0, n])
        place_in = lax.broadcasted_iota(jnp.int32, value.shape, 0)
        ok = jnp.logical_or(
            jnp.logical_and(place_in == 0, left), jnp.logical_and(place_in == 1, right)
        )
        value = jnp.where(ok, value, 0.0)
        for q, col in enumerate((-1, cols)):
            at = place * span + TILE + col
            put(ins, (slice(at, at + 1),), value[q : q + 1])
        leave[n, :cols] = take(ins, (inside(place),)).astype(bf16)
        leave[n, cols:] = value.astype(bf16)

    for n in range(2):

        @pl.when(row_there[n])
        def _():
            onward(n).start()

    def finish(n, back):
        for t in range(step):
            at = pl.ds(n * cols + t, TILE, stride=step)
            put(outs, (at,), back[t * TILE : (t + 1) * TILE])
        value = take(outs, (slice(n * cols, (n + 1) * cols),)) * gain[n]
        o_ref[0, n] = (value + xg[1, n].astype(f32)).astype(bf16)

    for place in (0, rows - 1):
        inner_tiles(place, place + 1)
    for q, place in halves:
        back = contract(k1t, every, [body(icat, place, half, 0, cols)])
        for at in range(half):
            n, part = place + at, slice(at * cols, (at + 1) * cols)
            if n in (0, rows - 1):
                out_edge[n // (rows - 1)] = back[part]
            else:
                finish(n, back[part])

    for n in range(2):

        @pl.when(row_there[n])
        def _():
            onward(1 - n).wait_recv()

    for n, (h, place, tap) in enumerate(edges):
        value = jnp.where(row_there[n], enter[n].astype(f32), 0.0)
        put(ins, (inside(place),), value[:cols])
        for q, col in enumerate((-1, cols)):
            at = place * span + TILE + col
            put(ins, (slice(at, at + 1),), value[cols + q : cols + q + 1])
        inner_tiles(place, h)
        back = contract(k1t, (tap,), [body(icat, place, 1, 0, cols)])
        finish(place, back + out_edge[n])

    for n in range(2):

        @pl.when(row_there[n])
        def _():
            row_both(n).wait_send()
            corner_copy(n).wait_send()
            onward(n).wait_send()

        @pl.when(col_there[n])
        def _():
            for m in range(2):
                col_copy(n, m).wait_send()


def hand_over(source, target, sem):
    copy = pltpu.make_async_copy(source, target, sem)
    copy.start()
    copy.wait()


def per_device(
    image_in,
    cotangent,
    first_kernel,
    first_bias,
    second_kernel,
    first_center,
    first_inverse,
    first_gain,
    first_shift,
    second_center,
    second_inverse,
    second_gain,
    second_shift,
):
    _, rows, cols, chans = image_in.shape
    groups = first_center.shape[0]
    span, step = cols + 2 * TILE, cols // TILE
    lanes = chans // LANES
    bf16, f32 = jnp.bfloat16, jnp.float32
    vec = lambda v: v.reshape(1, chans)
    result = pl.pallas_call(
        functools.partial(kernel, rows, cols, chans, groups),
        out_shape=jax.ShapeDtypeStruct(image_in.shape, bf16),
        in_specs=[pl.BlockSpec(memory_space=pltpu.HBM)] * 13,
        out_specs=pl.BlockSpec(memory_space=pltpu.VMEM),
        scratch_shapes=[
            pltpu.VMEM((2, rows, cols, chans), bf16),
            pltpu.VMEM((3, 3, chans, chans), bf16),
            pltpu.VMEM((3, 3, chans, chans), bf16),
            pltpu.VMEM((3, 3, chans, chans), bf16),
            pltpu.VMEM((3, 3, chans, chans), bf16),
            pltpu.VMEM((5, 1, chans), f32),
            pltpu.SMEM((4, groups), f32),
            pltpu.VMEM((4, 1, chans), f32),
            pltpu.VMEM((2, lanes, (rows + 2) * span, LANES), f32),
            pltpu.VMEM((lanes, rows * span, LANES), f32),
            pltpu.VMEM((lanes, rows * cols, LANES), f32),
            pltpu.VMEM((rows, cols, chans), f32),
            pltpu.VMEM((2, rows + 2, (step + 2) * TILE, chans), bf16),
            pltpu.VMEM((2, 9, 2 * TILE, chans), bf16),
            pltpu.VMEM((2, 2, 3, TILE, chans), f32),
            pltpu.VMEM((rows + 2, (step + 2) * TILE, chans), bf16),
            pltpu.VMEM((rows, cols, chans), f32),
            pltpu.VMEM((2 * TILE, chans), f32),
            pltpu.VMEM((2, cols, chans), f32),
            pltpu.VMEM((2, 2, TILE, chans), f32),
            pltpu.VMEM((2, cols, chans), f32),
            pltpu.VMEM((2, 2, cols, chans), bf16),
            pltpu.VMEM((2, 2, NEAR * rows, chans), bf16),
            pltpu.VMEM((2, 2, NEAR * rows, chans), bf16),
            pltpu.VMEM((2, TILE, chans), f32),
            pltpu.VMEM((2, TILE, chans), bf16),
            pltpu.VMEM((2, TILE, chans), bf16),
            pltpu.VMEM((2, cols + TILE, chans), bf16),
            pltpu.VMEM((2, cols + TILE, chans), bf16),
            pltpu.SemaphoreType.DMA((9,)),
            pltpu.SemaphoreType.DMA((2,)),
            pltpu.SemaphoreType.DMA((2,)),
            pltpu.SemaphoreType.DMA((2, 2)),
            pltpu.SemaphoreType.DMA((2, 2)),
            pltpu.SemaphoreType.DMA((2,)),
            pltpu.SemaphoreType.DMA((2,)),
            pltpu.SemaphoreType.DMA((2,)),
            pltpu.SemaphoreType.DMA((2,)),
        ],
        compiler_params=pltpu.CompilerParams(
            collective_id=0, has_side_effects=True, vmem_limit_bytes=40 << 20
        ),
    )(
        *(
            pltpu.with_memory_space_constraint(value, pltpu.HBM)
            for value in (
                image_in,
                cotangent,
                first_kernel,
                vec(first_bias),
                second_kernel,
                first_center,
                first_inverse,
                vec(first_gain),
                vec(first_shift),
                second_center,
                second_inverse,
                vec(second_gain),
                vec(second_shift),
            )
        )
    )
    return pl.pallas_call(
        hand_over,
        out_shape=jax.ShapeDtypeStruct(image_in.shape, bf16),
        in_specs=[pl.BlockSpec(memory_space=pltpu.VMEM)],
        out_specs=pl.BlockSpec(memory_space=pltpu.HBM),
        scratch_shapes=[pltpu.SemaphoreType.DMA],
        compiler_params=pltpu.CompilerParams(vmem_limit_bytes=8 << 20),
    )(result)


def solution(mesh):
    return jax.shard_map(
        per_device,
        mesh=mesh,
        in_specs=(P(None, "rows", "cols", None),) * 2 + (P(),) * 11,
        out_specs=P(None, "rows", "cols", None),
        check_vma=False,
    )
```

```python
import functools

import jax
import jax.numpy as jnp
from jax import lax
from jax.experimental import pallas as pl
from jax.experimental.pallas import tpu as pltpu
from jax.sharding import PartitionSpec as P

MESH = pl.DeviceIdType.MESH
TILE = 16
LANES = 128
NEAR = 2
SIDES = (-1, 1)


def kernel(
    rows,
    cols,
    chans,
    groups,
    x_hbm,
    g_hbm,
    k1_hbm,
    b1_hbm,
    k2_hbm,
    c1_hbm,
    v1_hbm,
    n1_hbm,
    s1_hbm,
    c2_hbm,
    v2_hbm,
    n2_hbm,
    s2_hbm,
    o_ref,
    xg,
    k1,
    k2,
    k1t,
    k2t,
    vecs,
    scal,
    params,
    stage,
    ins,
    outs,
    gain,
    cat,
    edge_cat,
    icat,
    back_main,
    pre_main,
    back_part,
    pre_part,
    out_edge,
    row_halo,
    pack,
    col_halo,
    corner_f32,
    corner_out,
    corner_in,
    load_sem,
    row_send,
    row_recv,
    col_send,
    col_recv,
    corner_send,
    corner_recv,
):
    span = cols + 2 * TILE
    step = cols // TILE
    lane_parts = [slice(k, k + LANES) for k in range(0, chans, LANES)]
    f32, bf16 = jnp.float32, jnp.bfloat16
    my_row, my_col = lax.axis_index("rows"), lax.axis_index("cols")
    n_rows, n_cols = lax.axis_size("rows"), lax.axis_size("cols")
    above, below = my_row > 0, my_row < n_rows - 1
    left, right = my_col > 0, my_col < n_cols - 1
    row_there, col_there = (above, below), (left, right)

    barrier = pltpu.get_barrier_semaphore()
    for n, side in enumerate(SIDES):

        @pl.when(col_there[n])
        def _():
            pl.semaphore_signal(
                barrier, inc=1, device_id=(my_row, my_col + side), device_id_type=MESH
            )

        @pl.when(row_there[n])
        def _():
            pl.semaphore_signal(
                barrier, inc=1, device_id=(my_row + side, my_col), device_id_type=MESH
            )

    load_k2 = pltpu.make_async_copy(k2_hbm, k2, load_sem.at[0])
    load_k1 = pltpu.make_async_copy(k1_hbm, k1, load_sem.at[1])
    load_x = pltpu.make_async_copy(x_hbm.at[0], xg.at[0], load_sem.at[2])
    load_g = pltpu.make_async_copy(g_hbm.at[0], xg.at[1], load_sem.at[3])
    load_g.start()
    load_x.start()
    for n, ref in enumerate((b1_hbm, n1_hbm, s1_hbm, n2_hbm, s2_hbm)):
        pltpu.make_async_copy(ref, vecs.at[n], load_sem.at[4]).start()
    for n, ref in enumerate((c1_hbm, v1_hbm, c2_hbm, v2_hbm)):
        pltpu.make_async_copy(ref, scal.at[n], load_sem.at[5 + n]).start()
    load_k2.start()
    load_k1.start()

    def one(there):
        return jnp.where(there, 1, 0)


    def row_link(n, d, src, dst):
        return pltpu.make_async_remote_copy(
            src_ref=src,
            dst_ref=dst,
            send_sem=row_send.at[n, d],
            recv_sem=row_recv.at[1 - n, d],
            device_id=(my_row + SIDES[n], my_col),
            device_id_type=MESH,
        )

    def send_rows(d, which):
        for n in range(2):

            @pl.when(row_there[n])
            def _():
                for m in which:
                    src = (x_hbm, g_hbm)[m].at[0, (d, rows - 1 - d)[n]]
                    row_link(n, d, src, row_halo.at[1 - n, d, m]).start()

    def row_both(n, d):
        return row_link(n, d, row_halo.at[1 - n, d], row_halo.at[1 - n, d])

    def col_copy(n, m):
        return pltpu.make_async_remote_copy(
            src_ref=pack.at[n, m],
            dst_ref=col_halo.at[1 - n, m],
            send_sem=col_send.at[n, m],
            recv_sem=col_recv.at[1 - n, m],
            device_id=(my_row, my_col + SIDES[n]),
            device_id_type=MESH,
        )

    def corner_copy(n):
        return pltpu.make_async_remote_copy(
            src_ref=corner_out.at[n],
            dst_ref=corner_in.at[1 - n],
            send_sem=corner_send.at[n],
            recv_sem=corner_recv.at[1 - n],
            device_id=(my_row + SIDES[n], my_col),
            device_id_type=MESH,
        )


    def flip(source, target):
        for i in range(3):
            for j in range(3):
                target[i, j] = source[2 - i, 2 - j].T

    def put(ref, at, value):
        for k, lanes in enumerate(lane_parts):
            ref[(*at[:-1], k, at[-1])] = value[:, lanes]

    def take(ref, at):
        return jnp.concatenate([ref[(*at[:-1], k, at[-1])] for k in range(len(lane_parts))], 1)

    def near(h, n):
        first = h * span + (TILE - NEAR, TILE + cols)[n]
        return slice(first, first + NEAR)

    def inside(h):
        return slice(h * span + TILE, h * span + TILE + cols)

    def down(h, col):
        return pl.ds(h * span + TILE + col, rows, stride=span)

    def tiles(m, h, which):
        for t in which:
            part = take(stage, (m, pl.ds(h * span + TILE + t - 1, TILE, stride=step)))
            cat[m, h, t * TILE : (t + 1) * TILE] = part.astype(bf16)

    def pack_cols(m):
        for n in range(2):
            for c in range(NEAR):
                part = take(stage, (m, down(2, (0, cols - NEAR)[n] + c)))
                pack[n, m, c * rows : (c + 1) * rows] = part.astype(bf16)

    def send_cols(m):
        for n in range(2):

            @pl.when(col_there[n])
            def _():
                col_copy(n, m).start()

    for h in (0, rows + 1):
        icat[h] = jnp.zeros(icat.shape[1:], bf16)
    for h in (0, rows + 3):
        for m in range(2):
            cat[m, h] = jnp.zeros(cat.shape[2:], bf16)
    edge_cat[...] = jnp.zeros(edge_cat.shape, f32)

    load_g.wait()
    for n in range(rows):
        put(stage, (1, inside(n + 2)), xg[1, n].astype(f32))
    pack_cols(1)
    pltpu.make_async_copy(vecs, vecs, load_sem.at[4]).wait()
    for n, ref in enumerate((c1_hbm, v1_hbm, c2_hbm, v2_hbm)):
        pltpu.make_async_copy(ref, scal.at[n], load_sem.at[5 + n]).wait()
    lane_group = lax.broadcasted_iota(jnp.int32, (1, chans), 1) // (chans // groups)

    def spread(n):
        total = jnp.zeros((1, chans), f32)
        for q in range(groups):
            total = jnp.where(lane_group == q, scal[n, q], total)
        return total

    scale1 = spread(1) * vecs[1]
    scale2 = spread(3) * vecs[3]
    params[0] = 0.5 * scale1
    params[1] = 0.5 * (vecs[2] - spread(0) * scale1)
    params[2] = 0.5 * scale2
    params[3] = 0.5 * ((vecs[0] - spread(2)) * scale2 + vecs[4])

    pl.semaphore_wait(barrier, one(above) + one(below) + one(left) + one(right))
    send_rows(0, (1,))
    send_cols(1)

    def activate(value):
        half_pre = value.astype(f32) * params[0] + params[1]
        return half_pre * (1.0 + jnp.tanh(half_pre))

    load_x.wait()
    for n in range(rows):
        half_pre = xg[0, n].astype(f32) * params[0] + params[1]
        more = 1.0 + jnp.tanh(half_pre)
        act = half_pre * more
        put(stage, (0, inside(n + 2)), act)
        gain[n] = (1.0 + half_pre + half_pre - act) * (more * params[0])
    pack_cols(0)
    send_cols(0)
    send_rows(0, (0,))

    def slope(half_pre, factor):
        tanh = jnp.tanh(half_pre)
        return (1.0 + half_pre * (1.0 - tanh)) * ((1.0 + tanh) * factor)

    def inner_value(back, pre):
        return slope(pre * params[2] + params[3], back * params[2])

    every = (0, 1, 2)

    def contract(weights, taps, pieces):
        lhs = []
        for i in taps:
            for j in range(3):
                stack = [part for piece in pieces for part in piece(i, j)]
                lhs.append(stack[0] if len(stack) == 1 else jnp.concatenate(stack, 0))
        rhs = weights[taps[0] : taps[-1] + 1].reshape(len(taps) * 3 * chans, chans)
        return jnp.dot(jnp.concatenate(lhs, 1), rhs, preferred_element_type=f32)

    def body(ref, place, count, start, width):
        def piece(i, j):
            part = ref[place + i : place + i + count, (start + j) * TILE : (start + j) * TILE + width]
            return [part.reshape(count * width, chans)]

        return piece

    half = (rows - 2) // 2
    halves = ((2, half), (2 + half, rows - 2 - half))

    def inner_store(ref, n, value):
        for t in range(step):
            at = pl.ds(n * span + TILE + t, TILE, stride=step)
            put(ref, (at,), value[t * TILE : (t + 1) * TILE])

    def inner_tiles(ref, n, h):
        for t in range(step + 2):
            part = take(ref, (pl.ds(n * span + TILE + t - 1, TILE, stride=step),))
            icat[h, t * TILE : (t + 1) * TILE] = part.astype(bf16)

    def products(place, count):
        back = contract(k2t, every, [body(cat.at[1], place, count, 0, cols)])
        pre = contract(k1, every, [body(cat.at[0], place, count, 0, cols)])
        for n in range(count):
            back_main[place + n] = back[n * cols : (n + 1) * cols]
            pre_main[place + n] = pre[n * cols : (n + 1) * cols]

    def inner_rows(place, count):
        for n in range(place, place + count):
            inner_store(ins, n, inner_value(back_main[n], pre_main[n]))

    load_k2.wait()
    load_k1.wait()
    flip(k2, k2t)
    for h in range(2, rows + 2):
        for m in range(2):
            tiles(m, h, range(step + 2))
    products(*halves[0])

    for m in (1, 0):
        for n in range(2):

            @pl.when(col_there[n])
            def _():
                col_copy(1 - n, m).wait_recv()

    for m in range(2):
        for n in range(2):
            for c in range(NEAR):
                part = col_halo[n, m, c * rows : (c + 1) * rows].astype(f32)
                part = jnp.where(col_there[n], part, 0.0)
                put(stage, (m, down(2, (-NEAR, cols)[n] + c)), part)
    def corner_at(d, m, q):
        first = ((2 * d + m) * 2 + q) * NEAR
        return slice(first, first + NEAR)

    for n in range(2):
        for d in range(2):
            for m in range(2):
                for q in range(2):
                    h = (2 + d, rows + 1 - d)[n]
                    corner_f32[n, corner_at(d, m, q)] = take(stage, (m, near(h, q)))
        corner_out[n] = corner_f32[n].astype(bf16)
    for n in range(2):

        @pl.when(row_there[n])
        def _():
            corner_copy(n).start()

    send_rows(1, (1, 0))

    products(*halves[1])
    inner_rows(*halves[0])
    flip(k1, k1t)
    def out_store(at, back):
        for t in range(step):
            put(outs, (pl.ds(at + t, TILE, stride=step),), back[t * TILE : (t + 1) * TILE])

    def finish(n):
        value = take(outs, (slice(n * cols, (n + 1) * cols),)) * gain[n]
        o_ref[0, n] = (value + xg[1, n].astype(f32)).astype(bf16)

    side_cols = (-1, 0, cols - 1, cols)

    def beside(m):
        return lambda i, j: [
            take(stage, (m, down(i + 1, col + j - 1))).astype(bf16) for col in side_cols
        ]

    value = inner_value(contract(k2t, every, [beside(1)]), contract(k1, every, [beside(0)]))
    inner_rows(*halves[1])
    for q, (col, there) in enumerate(zip(side_cols, (left, None, None, right))):
        part = value[q * TILE : q * TILE + rows]
        put(ins, (down(1, col),), part if there is None else jnp.where(there, part, 0.0))
    for n in range(2, rows):
        inner_tiles(ins, n, n)

    half = (rows - 4) // 2
    for place in (2, 2 + half):
        back = contract(k1t, every, [body(icat, place, half, 0, cols)])
        for q in range(half):
            out_store((place + q) * cols, back[q * cols : (q + 1) * cols])

    for n in range(2):

        @pl.when(row_there[n])
        def _():
            row_both(1 - n, 0).wait_recv()
            corner_copy(1 - n).wait_recv()

    def ends_at(h, j):
        return pl.ds(h * span + TILE + j - 2, 2, stride=cols + 1)

    def edge_tiles(n, h):
        for m in range(2):
            for j in range(3):
                place = h - n * rows
                edge_cat[n, m, place, j, :2] = take(stage, (m, ends_at(h, j)))

    def stage_halo(n, d):
        h = (1 - d, rows + 2 + d)[n]
        for m in range(2):
            value = row_halo[n, d, m]
            value = value.astype(f32) if m else activate(value)
            put(stage, (m, inside(h)), jnp.where(row_there[n], value, 0.0))
            for q in range(2):
                put(stage, (m, near(h, q)), corner_f32[n, corner_at(d, m, q)])
            tiles(m, h, range(step + 2))
        edge_tiles(n, h)

    def line(n, m, place):
        def piece(i, j):
            ends = edge_cat[n, m, place + i - n * rows, j].astype(bf16)
            return [cat[m, place + i, j * TILE : j * TILE + cols], ends]

        return piece

    place_in = lax.broadcasted_iota(jnp.int32, (TILE, chans), 0)
    ends_ok = jnp.logical_or(
        jnp.logical_and(place_in == 0, left), jnp.logical_and(place_in == 1, right)
    )

    def edge_store(place, value, there=None):
        main, ends = value[:cols], jnp.where(ends_ok, value[cols:], 0.0)
        if there is not None:
            main, ends = jnp.where(there, main, 0.0), jnp.where(there, ends, 0.0)
        inner_store(ins, place, main)
        for q, col in enumerate((-1, cols)):
            at = place * span + TILE + col
            put(ins, (slice(at, at + 1),), ends[q : q + 1])
        inner_tiles(ins, place, place)

    for n in range(2):
        corner_f32[n] = jnp.where(row_there[n], corner_in[n].astype(f32), 0.0)
        stage_halo(n, 0)
        for h in ((2, 3), (rows, rows + 1))[n]:
            for m in range(2):
                tiles(m, h, (0, step + 1))
            edge_tiles(n, h)
    wide = cols + TILE
    places = ((0, 1), (rows + 1, rows))
    lines = [[line(n, m, place) for n in range(2) for place in places[n]] for m in range(2)]
    back = contract(k2t, every, lines[1])
    pre = contract(k1, every, lines[0])
    for n in range(2, rows - 2):
        finish(n)
    for n, (outer, place) in enumerate(places):
        first = 2 * n * wide
        back_part[n] = back[first : first + wide]
        pre_part[n] = pre[first : first + wide]
        first += wide
        edge_store(place, inner_value(back[first : first + wide], pre[first : first + wide]))

    for n, place in enumerate((0, rows - 2)):
        back = contract(k1t, every, [body(icat, place, 2, 0, cols)])
        out_edge[n] = back[n * cols : (n + 1) * cols]
        inner = (1, rows - 2)[n]
        out_store(inner * cols, back[(1 - n) * cols : (2 - n) * cols])
        finish(inner)

    for n in range(2):

        @pl.when(row_there[n])
        def _():
            row_both(1 - n, 1).wait_recv()

    for n in range(2):
        stage_halo(n, 1)
    for n, (outer, tap) in enumerate(((0, 0), (rows + 1, 2))):
        back = contract(k2t, (tap,), [line(n, 1, outer)]) + back_part[n]
        pre = contract(k1, (tap,), [line(n, 0, outer)]) + pre_part[n]
        edge_store(outer, inner_value(back, pre), row_there[n])
    for n, (outer, place, tap) in enumerate(((0, 0, 0), (rows + 1, rows - 1, 2))):
        back = contract(k1t, (tap,), [body(icat, place, 1, 0, cols)])
        out_store(place * cols, back + out_edge[n])
        finish(place)

    for n in range(2):

        @pl.when(row_there[n])
        def _():
            for d in range(2):
                row_both(n, d).wait_send()
            corner_copy(n).wait_send()

        @pl.when(col_there[n])
        def _():
            for m in range(2):
                col_copy(n, m).wait_send()


def hand_over(source, target, sem):
    copy = pltpu.make_async_copy(source, target, sem)
    copy.start()
    copy.wait()


def per_device(
    image_in,
    cotangent,
    first_kernel,
    first_bias,
    second_kernel,
    first_center,
    first_inverse,
    first_gain,
    first_shift,
    second_center,
    second_inverse,
    second_gain,
    second_shift,
):
    _, rows, cols, chans = image_in.shape
    groups = first_center.shape[0]
    span, step = cols + 2 * TILE, cols // TILE
    lanes = chans // LANES
    bf16, f32 = jnp.bfloat16, jnp.float32
    vec = lambda v: v.reshape(1, chans)
    result = pl.pallas_call(
        functools.partial(kernel, rows, cols, chans, groups),
        out_shape=jax.ShapeDtypeStruct(image_in.shape, bf16),
        in_specs=[pl.BlockSpec(memory_space=pltpu.HBM)] * 13,
        out_specs=pl.BlockSpec(memory_space=pltpu.VMEM),
        scratch_shapes=[
            pltpu.VMEM((2, rows, cols, chans), bf16),
            pltpu.VMEM((3, 3, chans, chans), bf16),
            pltpu.VMEM((3, 3, chans, chans), bf16),
            pltpu.VMEM((3, 3, chans, chans), bf16),
            pltpu.VMEM((3, 3, chans, chans), bf16),
            pltpu.VMEM((5, 1, chans), f32),
            pltpu.SMEM((4, groups), f32),
            pltpu.VMEM((4, 1, chans), f32),
            pltpu.VMEM((2, lanes, (rows + 4) * span, LANES), f32),
            pltpu.VMEM((lanes, (rows + 2) * span, LANES), f32),
            pltpu.VMEM((lanes, rows * cols, LANES), f32),
            pltpu.VMEM((rows, cols, chans), f32),
            pltpu.VMEM((2, rows + 4, (step + 2) * TILE, chans), bf16),
            pltpu.VMEM((2, 2, 4, 3, TILE, chans), f32),
            pltpu.VMEM((rows + 2, (step + 2) * TILE, chans), bf16),
            pltpu.VMEM((rows + 2, cols, chans), f32),
            pltpu.VMEM((rows + 2, cols, chans), f32),
            pltpu.VMEM((2, cols + TILE, chans), f32),
            pltpu.VMEM((2, cols + TILE, chans), f32),
            pltpu.VMEM((2, cols, chans), f32),
            pltpu.VMEM((2, 2, 2, cols, chans), bf16),
            pltpu.VMEM((2, 2, NEAR * rows, chans), bf16),
            pltpu.VMEM((2, 2, NEAR * rows, chans), bf16),
            pltpu.VMEM((2, TILE, chans), f32),
            pltpu.VMEM((2, TILE, chans), bf16),
            pltpu.VMEM((2, TILE, chans), bf16),
            pltpu.SemaphoreType.DMA((9,)),
            pltpu.SemaphoreType.DMA((2, 2)),
            pltpu.SemaphoreType.DMA((2, 2)),
            pltpu.SemaphoreType.DMA((2, 2)),
            pltpu.SemaphoreType.DMA((2, 2)),
            pltpu.SemaphoreType.DMA((2,)),
            pltpu.SemaphoreType.DMA((2,)),
        ],
        compiler_params=pltpu.CompilerParams(
            collective_id=0, has_side_effects=True, vmem_limit_bytes=40 << 20
        ),
    )(
        *(
            pltpu.with_memory_space_constraint(value, pltpu.HBM)
            for value in (
                image_in,
                cotangent,
                first_kernel,
                vec(first_bias),
                second_kernel,
                first_center,
                first_inverse,
                vec(first_gain),
                vec(first_shift),
                second_center,
                second_inverse,
                vec(second_gain),
                vec(second_shift),
            )
        )
    )
    return pl.pallas_call(
        hand_over,
        out_shape=jax.ShapeDtypeStruct(image_in.shape, bf16),
        in_specs=[pl.BlockSpec(memory_space=pltpu.VMEM)],
        out_specs=pl.BlockSpec(memory_space=pltpu.HBM),
        scratch_shapes=[pltpu.SemaphoreType.DMA],
        compiler_params=pltpu.CompilerParams(vmem_limit_bytes=8 << 20),
    )(result)


def solution(mesh):
    return jax.shard_map(
        per_device,
        mesh=mesh,
        in_specs=(P(None, "rows", "cols", None),) * 2 + (P(),) * 11,
        out_specs=P(None, "rows", "cols", None),
        check_vma=False,
    )
```

```python
import functools

import jax
import jax.numpy as jnp
from jax import lax
from jax.experimental import pallas as pl
from jax.experimental.pallas import tpu as pltpu
from jax.sharding import PartitionSpec as P

MESH = pl.DeviceIdType.MESH
TILE = 16
LANES = 128
NEAR = 2
SIDES = (-1, 1)


def kernel(
    rows,
    cols,
    chans,
    groups,
    x_hbm,
    g_hbm,
    k1_hbm,
    b1_hbm,
    k2_hbm,
    c1_hbm,
    v1_hbm,
    n1_hbm,
    s1_hbm,
    c2_hbm,
    v2_hbm,
    n2_hbm,
    s2_hbm,
    o_ref,
    xg,
    k1,
    k2,
    k1t,
    k2t,
    vecs,
    scal,
    params,
    stage,
    raw,
    ins,
    outs,
    gain,
    cat,
    edge_cat,
    icat,
    back_main,
    pre_main,
    back_part,
    pre_part,
    out_edge,
    row_halo,
    pack,
    col_halo,
    corner_f32,
    corner_out,
    corner_in,
    load_sem,
    row_send,
    row_recv,
    col_send,
    col_recv,
    corner_send,
    corner_recv,
):
    span = cols + 2 * TILE
    step = cols // TILE
    lane_parts = [slice(k, k + LANES) for k in range(0, chans, LANES)]
    f32, bf16 = jnp.float32, jnp.bfloat16
    my_row, my_col = lax.axis_index("rows"), lax.axis_index("cols")
    n_rows, n_cols = lax.axis_size("rows"), lax.axis_size("cols")
    above, below = my_row > 0, my_row < n_rows - 1
    left, right = my_col > 0, my_col < n_cols - 1
    row_there, col_there = (above, below), (left, right)

    barrier = pltpu.get_barrier_semaphore()
    for n, side in enumerate(SIDES):

        @pl.when(col_there[n])
        def _():
            pl.semaphore_signal(
                barrier, inc=1, device_id=(my_row, my_col + side), device_id_type=MESH
            )

        @pl.when(row_there[n])
        def _():
            pl.semaphore_signal(
                barrier, inc=1, device_id=(my_row + side, my_col), device_id_type=MESH
            )

    load_k2 = pltpu.make_async_copy(k2_hbm, k2, load_sem.at[0])
    load_k1 = pltpu.make_async_copy(k1_hbm, k1, load_sem.at[1])
    load_x = pltpu.make_async_copy(x_hbm.at[0], xg.at[0], load_sem.at[2])
    load_g = pltpu.make_async_copy(g_hbm.at[0], xg.at[1], load_sem.at[3])
    load_g.start()
    load_x.start()
    for n, ref in enumerate((b1_hbm, n1_hbm, s1_hbm, n2_hbm, s2_hbm)):
        pltpu.make_async_copy(ref, vecs.at[n], load_sem.at[4]).start()
    for n, ref in enumerate((c1_hbm, v1_hbm, c2_hbm, v2_hbm)):
        pltpu.make_async_copy(ref, scal.at[n], load_sem.at[5 + n]).start()
    load_k2.start()
    load_k1.start()

    def one(there):
        return jnp.where(there, 1, 0)


    def row_link(n, d, src, dst):
        return pltpu.make_async_remote_copy(
            src_ref=src,
            dst_ref=dst,
            send_sem=row_send.at[n, d],
            recv_sem=row_recv.at[1 - n, d],
            device_id=(my_row + SIDES[n], my_col),
            device_id_type=MESH,
        )

    def send_rows(d, which):
        for n in range(2):

            @pl.when(row_there[n])
            def _():
                for m in which:
                    src = (x_hbm, g_hbm)[m].at[0, (d, rows - 1 - d)[n]]
                    row_link(n, d, src, row_halo.at[1 - n, d, m]).start()

    def row_both(n, d):
        return row_link(n, d, row_halo.at[1 - n, d], row_halo.at[1 - n, d])

    def col_copy(n, m):
        return pltpu.make_async_remote_copy(
            src_ref=pack.at[n, m],
            dst_ref=col_halo.at[1 - n, m],
            send_sem=col_send.at[n, m],
            recv_sem=col_recv.at[1 - n, m],
            device_id=(my_row, my_col + SIDES[n]),
            device_id_type=MESH,
        )

    def corner_copy(n):
        return pltpu.make_async_remote_copy(
            src_ref=corner_out.at[n],
            dst_ref=corner_in.at[1 - n],
            send_sem=corner_send.at[n],
            recv_sem=corner_recv.at[1 - n],
            device_id=(my_row + SIDES[n], my_col),
            device_id_type=MESH,
        )


    def flip(source, target):
        for i in range(3):
            for j in range(3):
                target[i, j] = source[2 - i, 2 - j].T

    def put(ref, at, value):
        for k, lanes in enumerate(lane_parts):
            ref[(*at[:-1], k, at[-1])] = value[:, lanes]

    def take(ref, at):
        return jnp.concatenate([ref[(*at[:-1], k, at[-1])] for k in range(len(lane_parts))], 1)

    def near(h, n):
        first = h * span + (TILE - NEAR, TILE + cols)[n]
        return slice(first, first + NEAR)

    def inside(h):
        return slice(h * span + TILE, h * span + TILE + cols)

    def down(h, col):
        return pl.ds(h * span + TILE + col, rows, stride=span)

    def tiles(m, h, which):
        for t in which:
            part = take(stage, (m, pl.ds(h * span + TILE + t - 1, TILE, stride=step)))
            cat[m, h, t * TILE : (t + 1) * TILE] = part.astype(bf16)

    def pack_cols(m):
        for n in range(2):
            for r in range(rows):
                tile = xg[m, r, (0, cols - TILE)[n] : (TILE, cols)[n]].astype(f32)
                put(raw, (n, m, slice(r * TILE, (r + 1) * TILE)), tile)
            for c in range(NEAR):
                column = pl.ds((0, TILE - NEAR)[n] + c, rows, stride=TILE)
                part = take(raw, (n, m, column))
                pack[n, m, c * rows : (c + 1) * rows] = part.astype(bf16)

    def send_cols(m):
        for n in range(2):

            @pl.when(col_there[n])
            def _():
                col_copy(n, m).start()

    for h in (0, rows + 1):
        icat[h] = jnp.zeros(icat.shape[1:], bf16)
    for h in (0, rows + 3):
        for m in range(2):
            cat[m, h] = jnp.zeros(cat.shape[2:], bf16)
    edge_cat[...] = jnp.zeros(edge_cat.shape, f32)

    load_g.wait()
    for n in range(rows):
        put(stage, (1, inside(n + 2)), xg[1, n].astype(f32))
    pack_cols(1)
    pltpu.make_async_copy(vecs, vecs, load_sem.at[4]).wait()
    for n, ref in enumerate((c1_hbm, v1_hbm, c2_hbm, v2_hbm)):
        pltpu.make_async_copy(ref, scal.at[n], load_sem.at[5 + n]).wait()
    lane_group = lax.broadcasted_iota(jnp.int32, (1, chans), 1) // (chans // groups)

    def spread(n):
        total = jnp.zeros((1, chans), f32)
        for q in range(groups):
            total = jnp.where(lane_group == q, scal[n, q], total)
        return total

    scale1 = spread(1) * vecs[1]
    scale2 = spread(3) * vecs[3]
    params[0] = 0.5 * scale1
    params[1] = 0.5 * (vecs[2] - spread(0) * scale1)
    params[2] = 0.5 * scale2
    params[3] = 0.5 * ((vecs[0] - spread(2)) * scale2 + vecs[4])

    pl.semaphore_wait(barrier, one(above) + one(below) + one(left) + one(right))
    send_rows(0, (1,))
    send_cols(1)
    load_x.wait()
    pack_cols(0)
    send_cols(0)
    send_rows(0, (0,))

    def activate(value):
        half_pre = value.astype(f32) * params[0] + params[1]
        return half_pre * (1.0 + jnp.tanh(half_pre))

    for n in range(rows):
        half_pre = xg[0, n].astype(f32) * params[0] + params[1]
        more = 1.0 + jnp.tanh(half_pre)
        act = half_pre * more
        put(stage, (0, inside(n + 2)), act)
        gain[n] = (1.0 + half_pre + half_pre - act) * (more * params[0])

    def slope(half_pre, factor):
        tanh = jnp.tanh(half_pre)
        return (1.0 + half_pre * (1.0 - tanh)) * ((1.0 + tanh) * factor)

    def inner_value(back, pre):
        return slope(pre * params[2] + params[3], back * params[2])

    every = (0, 1, 2)

    def contract(weights, taps, pieces):
        lhs = []
        for i in taps:
            for j in range(3):
                stack = [part for piece in pieces for part in piece(i, j)]
                lhs.append(stack[0] if len(stack) == 1 else jnp.concatenate(stack, 0))
        rhs = weights[taps[0] : taps[-1] + 1].reshape(len(taps) * 3 * chans, chans)
        return jnp.dot(jnp.concatenate(lhs, 1), rhs, preferred_element_type=f32)

    def body(ref, place, count, start, width):
        def piece(i, j):
            part = ref[place + i : place + i + count, (start + j) * TILE : (start + j) * TILE + width]
            return [part.reshape(count * width, chans)]

        return piece

    half = rows // 2
    halves = ((2, half), (2 + half, rows - 2 - half))

    def inner_store(ref, n, value):
        for t in range(step):
            at = pl.ds(n * span + TILE + t, TILE, stride=step)
            put(ref, (at,), value[t * TILE : (t + 1) * TILE])

    def inner_tiles(ref, n, h):
        for t in range(step + 2):
            part = take(ref, (pl.ds(n * span + TILE + t - 1, TILE, stride=step),))
            icat[h, t * TILE : (t + 1) * TILE] = part.astype(bf16)

    def products(place, count):
        back = contract(k2t, every, [body(cat.at[1], place, count, 0, cols)])
        pre = contract(k1, every, [body(cat.at[0], place, count, 0, cols)])
        for n in range(count):
            back_main[place + n] = back[n * cols : (n + 1) * cols]
            pre_main[place + n] = pre[n * cols : (n + 1) * cols]

    def inner_rows(place, count):
        for n in range(place, place + count):
            inner_store(ins, n, inner_value(back_main[n], pre_main[n]))

    load_k2.wait()
    load_k1.wait()
    flip(k2, k2t)
    for h in range(2, rows + 2):
        for m in range(2):
            tiles(m, h, range(step + 2))
    products(*halves[0])

    for m in (1, 0):
        for n in range(2):

            @pl.when(col_there[n])
            def _():
                col_copy(1 - n, m).wait_recv()

    for m in range(2):
        for n in range(2):
            for c in range(NEAR):
                part = col_halo[n, m, c * rows : (c + 1) * rows]
                part = part.astype(f32) if m else activate(part)
                part = jnp.where(col_there[n], part, 0.0)
                put(stage, (m, down(2, (-NEAR, cols)[n] + c)), part)
    def corner_at(d, m, q):
        first = ((2 * d + m) * 2 + q) * NEAR
        return slice(first, first + NEAR)

    for n in range(2):
        for d in range(2):
            for m in range(2):
                for q in range(2):
                    h = (2 + d, rows + 1 - d)[n]
                    corner_f32[n, corner_at(d, m, q)] = take(stage, (m, near(h, q)))
        corner_out[n] = corner_f32[n].astype(bf16)
    for n in range(2):

        @pl.when(row_there[n])
        def _():
            corner_copy(n).start()

    send_rows(1, (1, 0))

    products(*halves[1])
    inner_rows(*halves[0])
    flip(k1, k1t)
    def out_store(at, back):
        for t in range(step):
            put(outs, (pl.ds(at + t, TILE, stride=step),), back[t * TILE : (t + 1) * TILE])

    def finish(n):
        value = take(outs, (slice(n * cols, (n + 1) * cols),)) * gain[n]
        o_ref[0, n] = (value + xg[1, n].astype(f32)).astype(bf16)

    side_cols = (-1, 0, cols - 1, cols)

    def beside(m):
        return lambda i, j: [
            take(stage, (m, down(i + 1, col + j - 1))).astype(bf16) for col in side_cols
        ]

    value = inner_value(contract(k2t, every, [beside(1)]), contract(k1, every, [beside(0)]))
    inner_rows(*halves[1])
    for q, (col, there) in enumerate(zip(side_cols, (left, None, None, right))):
        part = value[q * TILE : q * TILE + rows]
        put(ins, (down(1, col),), part if there is None else jnp.where(there, part, 0.0))
    for n in range(2, rows):
        inner_tiles(ins, n, n)

    half = (rows - 4) // 2
    for place in (2, 2 + half):
        back = contract(k1t, every, [body(icat, place, half, 0, cols)])
        for q in range(half):
            out_store((place + q) * cols, back[q * cols : (q + 1) * cols])

    for n in range(2):

        @pl.when(row_there[n])
        def _():
            row_both(1 - n, 0).wait_recv()
            corner_copy(1 - n).wait_recv()

    def ends_at(h, j):
        return pl.ds(h * span + TILE + j - 2, 2, stride=cols + 1)

    def edge_tiles(n, h):
        for m in range(2):
            for j in range(3):
                place = h - n * rows
                edge_cat[n, m, place, j, :2] = take(stage, (m, ends_at(h, j)))

    def stage_halo(n, d):
        h = (1 - d, rows + 2 + d)[n]
        for m in range(2):
            value = row_halo[n, d, m]
            value = value.astype(f32) if m else activate(value)
            put(stage, (m, inside(h)), jnp.where(row_there[n], value, 0.0))
            for q in range(2):
                put(stage, (m, near(h, q)), corner_f32[n, corner_at(d, m, q)])
            tiles(m, h, range(step + 2))
        edge_tiles(n, h)

    def line(n, m, place):
        def piece(i, j):
            ends = edge_cat[n, m, place + i - n * rows, j].astype(bf16)
            return [cat[m, place + i, j * TILE : j * TILE + cols], ends]

        return piece

    place_in = lax.broadcasted_iota(jnp.int32, (TILE, chans), 0)
    ends_ok = jnp.logical_or(
        jnp.logical_and(place_in == 0, left), jnp.logical_and(place_in == 1, right)
    )

    def edge_store(place, value, there=None):
        main, ends = value[:cols], jnp.where(ends_ok, value[cols:], 0.0)
        if there is not None:
            main, ends = jnp.where(there, main, 0.0), jnp.where(there, ends, 0.0)
        inner_store(ins, place, main)
        for q, col in enumerate((-1, cols)):
            at = place * span + TILE + col
            put(ins, (slice(at, at + 1),), ends[q : q + 1])
        inner_tiles(ins, place, place)

    for n in range(2):
        corner_f32[n] = jnp.where(row_there[n], corner_in[n].astype(f32), 0.0)
        stage_halo(n, 0)
        for h in ((2, 3), (rows, rows + 1))[n]:
            for m in range(2):
                tiles(m, h, (0, step + 1))
            edge_tiles(n, h)
    wide = cols + TILE
    places = ((0, 1), (rows + 1, rows))
    lines = [[line(n, m, place) for n in range(2) for place in places[n]] for m in range(2)]
    back = contract(k2t, every, lines[1])
    pre = contract(k1, every, lines[0])
    for n in range(2, rows - 2):
        finish(n)
    for n, (outer, place) in enumerate(places):
        first = 2 * n * wide
        back_part[n] = back[first : first + wide]
        pre_part[n] = pre[first : first + wide]
        first += wide
        edge_store(place, inner_value(back[first : first + wide], pre[first : first + wide]))

    for n, place in enumerate((0, rows - 2)):
        back = contract(k1t, every, [body(icat, place, 2, 0, cols)])
        out_edge[n] = back[n * cols : (n + 1) * cols]
        inner = (1, rows - 2)[n]
        out_store(inner * cols, back[(1 - n) * cols : (2 - n) * cols])
        finish(inner)

    for n in range(2):

        @pl.when(row_there[n])
        def _():
            row_both(1 - n, 1).wait_recv()

    for n in range(2):
        stage_halo(n, 1)
    for n, (outer, tap) in enumerate(((0, 0), (rows + 1, 2))):
        back = contract(k2t, (tap,), [line(n, 1, outer)]) + back_part[n]
        pre = contract(k1, (tap,), [line(n, 0, outer)]) + pre_part[n]
        edge_store(outer, inner_value(back, pre), row_there[n])
    for n, (outer, place, tap) in enumerate(((0, 0, 0), (rows + 1, rows - 1, 2))):
        back = contract(k1t, (tap,), [body(icat, place, 1, 0, cols)])
        out_store(place * cols, back + out_edge[n])
        finish(place)

    for n in range(2):

        @pl.when(row_there[n])
        def _():
            for d in range(2):
                row_both(n, d).wait_send()
            corner_copy(n).wait_send()

        @pl.when(col_there[n])
        def _():
            for m in range(2):
                col_copy(n, m).wait_send()


def hand_over(source, target, sem):
    copy = pltpu.make_async_copy(source, target, sem)
    copy.start()
    copy.wait()


def per_device(
    image_in,
    cotangent,
    first_kernel,
    first_bias,
    second_kernel,
    first_center,
    first_inverse,
    first_gain,
    first_shift,
    second_center,
    second_inverse,
    second_gain,
    second_shift,
):
    _, rows, cols, chans = image_in.shape
    groups = first_center.shape[0]
    span, step = cols + 2 * TILE, cols // TILE
    lanes = chans // LANES
    bf16, f32 = jnp.bfloat16, jnp.float32
    vec = lambda v: v.reshape(1, chans)
    result = pl.pallas_call(
        functools.partial(kernel, rows, cols, chans, groups),
        out_shape=jax.ShapeDtypeStruct(image_in.shape, bf16),
        in_specs=[pl.BlockSpec(memory_space=pltpu.HBM)] * 13,
        out_specs=pl.BlockSpec(memory_space=pltpu.VMEM),
        scratch_shapes=[
            pltpu.VMEM((2, rows, cols, chans), bf16),
            pltpu.VMEM((3, 3, chans, chans), bf16),
            pltpu.VMEM((3, 3, chans, chans), bf16),
            pltpu.VMEM((3, 3, chans, chans), bf16),
            pltpu.VMEM((3, 3, chans, chans), bf16),
            pltpu.VMEM((5, 1, chans), f32),
            pltpu.SMEM((4, groups), f32),
            pltpu.VMEM((4, 1, chans), f32),
            pltpu.VMEM((2, lanes, (rows + 4) * span, LANES), f32),
            pltpu.VMEM((2, 2, lanes, rows * TILE, LANES), f32),
            pltpu.VMEM((lanes, (rows + 2) * span, LANES), f32),
            pltpu.VMEM((lanes, rows * cols, LANES), f32),
            pltpu.VMEM((rows, cols, chans), f32),
            pltpu.VMEM((2, rows + 4, (step + 2) * TILE, chans), bf16),
            pltpu.VMEM((2, 2, 4, 3, TILE, chans), f32),
            pltpu.VMEM((rows + 2, (step + 2) * TILE, chans), bf16),
            pltpu.VMEM((rows + 2, cols, chans), f32),
            pltpu.VMEM((rows + 2, cols, chans), f32),
            pltpu.VMEM((2, cols + TILE, chans), f32),
            pltpu.VMEM((2, cols + TILE, chans), f32),
            pltpu.VMEM((2, cols, chans), f32),
            pltpu.VMEM((2, 2, 2, cols, chans), bf16),
            pltpu.VMEM((2, 2, NEAR * rows, chans), bf16),
            pltpu.VMEM((2, 2, NEAR * rows, chans), bf16),
            pltpu.VMEM((2, TILE, chans), f32),
            pltpu.VMEM((2, TILE, chans), bf16),
            pltpu.VMEM((2, TILE, chans), bf16),
            pltpu.SemaphoreType.DMA((9,)),
            pltpu.SemaphoreType.DMA((2, 2)),
            pltpu.SemaphoreType.DMA((2, 2)),
            pltpu.SemaphoreType.DMA((2, 2)),
            pltpu.SemaphoreType.DMA((2, 2)),
            pltpu.SemaphoreType.DMA((2,)),
            pltpu.SemaphoreType.DMA((2,)),
        ],
        compiler_params=pltpu.CompilerParams(
            collective_id=0, has_side_effects=True, vmem_limit_bytes=40 << 20
        ),
    )(
        *(
            pltpu.with_memory_space_constraint(value, pltpu.HBM)
            for value in (
                image_in,
                cotangent,
                first_kernel,
                vec(first_bias),
                second_kernel,
                first_center,
                first_inverse,
                vec(first_gain),
                vec(first_shift),
                second_center,
                second_inverse,
                vec(second_gain),
                vec(second_shift),
            )
        )
    )
    return pl.pallas_call(
        hand_over,
        out_shape=jax.ShapeDtypeStruct(image_in.shape, bf16),
        in_specs=[pl.BlockSpec(memory_space=pltpu.VMEM)],
        out_specs=pl.BlockSpec(memory_space=pltpu.HBM),
        scratch_shapes=[pltpu.SemaphoreType.DMA],
        compiler_params=pltpu.CompilerParams(vmem_limit_bytes=8 << 20),
    )(result)


def solution(mesh):
    return jax.shard_map(
        per_device,
        mesh=mesh,
        in_specs=(P(None, "rows", "cols", None),) * 2 + (P(),) * 11,
        out_specs=P(None, "rows", "cols", None),
        check_vma=False,
    )
```

```python
import functools

import jax
import jax.numpy as jnp
from jax import lax
from jax.experimental import pallas as pl
from jax.experimental.pallas import tpu as pltpu
from jax.sharding import PartitionSpec as P

MESH = pl.DeviceIdType.MESH
TILE = 16
LANES = 128
NEAR = 2
SIDES = (-1, 1)


def kernel(
    rows,
    cols,
    chans,
    groups,
    x_hbm,
    g_hbm,
    k1_hbm,
    b1_hbm,
    k2_hbm,
    c1_hbm,
    v1_hbm,
    n1_hbm,
    s1_hbm,
    c2_hbm,
    v2_hbm,
    n2_hbm,
    s2_hbm,
    o_ref,
    xg,
    k1,
    k2,
    k1t,
    k2t,
    vecs,
    scal,
    params,
    stage,
    raw,
    far,
    ins,
    edge_ins,
    outs,
    edge_outs,
    gain,
    cat,
    edge_cat,
    icat,
    back_main,
    pre_main,
    back_part,
    pre_part,
    out_edge,
    row_halo,
    pack,
    col_halo,
    corner_f32,
    corner_out,
    corner_in,
    load_sem,
    row_send,
    row_recv,
    col_send,
    col_recv,
    corner_send,
    corner_recv,
):
    span = cols + 2 * TILE
    step = cols // TILE
    lane_parts = [slice(k, k + LANES) for k in range(0, chans, LANES)]
    f32, bf16 = jnp.float32, jnp.bfloat16
    my_row, my_col = lax.axis_index("rows"), lax.axis_index("cols")
    n_rows, n_cols = lax.axis_size("rows"), lax.axis_size("cols")
    above, below = my_row > 0, my_row < n_rows - 1
    left, right = my_col > 0, my_col < n_cols - 1
    row_there, col_there = (above, below), (left, right)

    barrier = pltpu.get_barrier_semaphore()
    for n, side in enumerate(SIDES):

        @pl.when(col_there[n])
        def _():
            pl.semaphore_signal(
                barrier, inc=1, device_id=(my_row, my_col + side), device_id_type=MESH
            )

        @pl.when(row_there[n])
        def _():
            pl.semaphore_signal(
                barrier, inc=1, device_id=(my_row + side, my_col), device_id_type=MESH
            )

    load_k2 = pltpu.make_async_copy(k2_hbm, k2, load_sem.at[0])
    load_k1 = pltpu.make_async_copy(k1_hbm, k1, load_sem.at[1])
    load_x = pltpu.make_async_copy(x_hbm.at[0], xg.at[0], load_sem.at[2])
    load_g = pltpu.make_async_copy(g_hbm.at[0], xg.at[1], load_sem.at[3])
    load_g.start()
    load_x.start()
    for n, ref in enumerate((b1_hbm, n1_hbm, s1_hbm, n2_hbm, s2_hbm)):
        pltpu.make_async_copy(ref, vecs.at[n], load_sem.at[4]).start()
    for n, ref in enumerate((c1_hbm, v1_hbm, c2_hbm, v2_hbm)):
        pltpu.make_async_copy(ref, scal.at[n], load_sem.at[5 + n]).start()
    load_k2.start()
    load_k1.start()

    def one(there):
        return jnp.where(there, 1, 0)


    def row_link(n, d, src, dst):
        return pltpu.make_async_remote_copy(
            src_ref=src,
            dst_ref=dst,
            send_sem=row_send.at[n, d],
            recv_sem=row_recv.at[1 - n, d],
            device_id=(my_row + 2 * n - 1, my_col),
            device_id_type=MESH,
        )

    def beyond(n):
        return jnp.logical_and(my_row + 2 * n >= 1, my_row + 2 * n < n_rows + 1)

    def send_row(n, d, which):
        @pl.when(beyond(n))
        def _():
            for m in which:
                src = (x_hbm, g_hbm)[m].at[0, d + n * (rows - 1 - 2 * d)]
                row_link(n, d, src, row_halo.at[1 - n, d, m]).start()

    sooner = my_row % 2
    later = 1 - sooner

    def row_both(n, d):
        return row_link(n, d, row_halo.at[1 - n, d], row_halo.at[1 - n, d])

    def col_copy(n, m):
        return pltpu.make_async_remote_copy(
            src_ref=pack.at[n, m],
            dst_ref=col_halo.at[1 - n, m],
            send_sem=col_send.at[n, m],
            recv_sem=col_recv.at[1 - n, m],
            device_id=(my_row, my_col + SIDES[n]),
            device_id_type=MESH,
        )

    def corner_copy(n):
        return pltpu.make_async_remote_copy(
            src_ref=corner_out.at[n],
            dst_ref=corner_in.at[1 - n],
            send_sem=corner_send.at[n],
            recv_sem=corner_recv.at[1 - n],
            device_id=(my_row + SIDES[n], my_col),
            device_id_type=MESH,
        )


    def flip(source, target):
        for i in range(3):
            for j in range(3):
                target[i, j] = source[2 - i, 2 - j].T

    def put(ref, at, value):
        for k, lanes in enumerate(lane_parts):
            ref[(*at[:-1], k, at[-1])] = value[:, lanes]

    def take(ref, at):
        return jnp.concatenate([ref[(*at[:-1], k, at[-1])] for k in range(len(lane_parts))], 1)

    def near(h, n):
        first = h * span + (TILE - NEAR, TILE + cols)[n]
        return slice(first, first + NEAR)

    def inside(h):
        return slice(h * span + TILE, h * span + TILE + cols)

    def down(h, col):
        return pl.ds(h * span + TILE + col, rows, stride=span)

    def tiles(m, h, which):
        for t in which:
            part = take(stage, (m, pl.ds(h * span + TILE + t - 1, TILE, stride=step)))
            cat[m, h, t * TILE : (t + 1) * TILE] = part.astype(bf16)

    def pack_cols(m):
        for n in range(2):
            for r in range(rows):
                tile = xg[m, r, (0, cols - TILE)[n] : (TILE, cols)[n]].astype(f32)
                put(raw, (n, m, slice(r * TILE, (r + 1) * TILE)), tile)
            for c in range(NEAR):
                column = pl.ds((0, TILE - NEAR)[n] + c, rows, stride=TILE)
                part = take(raw, (n, m, column))
                pack[n, m, c * rows : (c + 1) * rows] = part.astype(bf16)

    def send_cols(m):
        for n in range(2):

            @pl.when(col_there[n])
            def _():
                col_copy(n, m).start()

    for h in (0, rows + 1):
        icat[h] = jnp.zeros(icat.shape[1:], bf16)
    for h in (0, rows + 3):
        for m in range(2):
            cat[m, h] = jnp.zeros(cat.shape[2:], bf16)
    edge_cat[...] = jnp.zeros(edge_cat.shape, f32)

    load_g.wait()
    for n in range(rows):
        put(stage, (1, inside(n + 2)), xg[1, n].astype(f32))
    pack_cols(1)
    pltpu.make_async_copy(vecs, vecs, load_sem.at[4]).wait()
    for n, ref in enumerate((c1_hbm, v1_hbm, c2_hbm, v2_hbm)):
        pltpu.make_async_copy(ref, scal.at[n], load_sem.at[5 + n]).wait()
    lane_group = lax.broadcasted_iota(jnp.int32, (1, chans), 1) // (chans // groups)

    def spread(n):
        total = jnp.zeros((1, chans), f32)
        for q in range(groups):
            total = jnp.where(lane_group == q, scal[n, q], total)
        return total

    scale1 = spread(1) * vecs[1]
    scale2 = spread(3) * vecs[3]
    params[0] = 0.5 * scale1
    params[1] = 0.5 * (vecs[2] - spread(0) * scale1)
    params[2] = 0.5 * scale2
    params[3] = 0.5 * ((vecs[0] - spread(2)) * scale2 + vecs[4])

    pl.semaphore_wait(barrier, one(above) + one(below) + one(left) + one(right))
    for n in range(2):
        send_row(n, 0, (1,))
    send_cols(1)
    load_x.wait()
    pack_cols(0)
    send_cols(0)
    for n in range(2):
        send_row(n, 0, (0,))

    def activate(value):
        half_pre = value.astype(f32) * params[0] + params[1]
        return half_pre * (1.0 + jnp.tanh(half_pre))

    for n in range(rows):
        half_pre = xg[0, n].astype(f32) * params[0] + params[1]
        more = 1.0 + jnp.tanh(half_pre)
        act = half_pre * more
        put(stage, (0, inside(n + 2)), act)
        gain[n] = (1.0 + half_pre + half_pre - act) * (more * params[0])

    def slope(half_pre, factor):
        tanh = jnp.tanh(half_pre)
        return (1.0 + half_pre * (1.0 - tanh)) * ((1.0 + tanh) * factor)

    def inner_value(back, pre):
        return slope(pre * params[2] + params[3], back * params[2])

    every = (0, 1, 2)

    def contract(weights, taps, pieces):
        lhs = []
        for i in taps:
            for j in range(3):
                stack = [part for piece in pieces for part in piece(i, j)]
                lhs.append(stack[0] if len(stack) == 1 else jnp.concatenate(stack, 0))
        rhs = weights[taps[0] : taps[-1] + 1].reshape(len(taps) * 3 * chans, chans)
        return jnp.dot(jnp.concatenate(lhs, 1), rhs, preferred_element_type=f32)

    def body(ref, place, count, start, width):
        def piece(i, j):
            part = ref[place + i : place + i + count, (start + j) * TILE : (start + j) * TILE + width]
            return [part.reshape(count * width, chans)]

        return piece

    half = rows // 2
    halves = ((2, half), (2 + half, rows - 2 - half))

    def inner_store(ref, n, value):
        for t in range(step):
            at = pl.ds(n * span + TILE + t, TILE, stride=step)
            put(ref, (at,), value[t * TILE : (t + 1) * TILE])

    def inner_tiles(ref, n, h):
        for t in range(step + 2):
            part = take(ref, (pl.ds(n * span + TILE + t - 1, TILE, stride=step),))
            icat[h, t * TILE : (t + 1) * TILE] = part.astype(bf16)

    def products(place, count):
        back = contract(k2t, every, [body(cat.at[1], place, count, 0, cols)])
        pre = contract(k1, every, [body(cat.at[0], place, count, 0, cols)])
        for n in range(count):
            back_main[place + n] = back[n * cols : (n + 1) * cols]
            pre_main[place + n] = pre[n * cols : (n + 1) * cols]

    def inner_rows(place, count):
        for n in range(place, place + count):
            inner_store(ins, n, inner_value(back_main[n], pre_main[n]))

    load_k2.wait()
    load_k1.wait()
    flip(k2, k2t)
    for h in range(2, rows + 2):
        for m in range(2):
            tiles(m, h, range(step + 2))
    products(*halves[0])

    for m in (1, 0):
        for n in range(2):

            @pl.when(col_there[n])
            def _():
                col_copy(1 - n, m).wait_recv()

    for m in range(2):
        for n in range(2):
            for c in range(NEAR):
                part = col_halo[n, m, c * rows : (c + 1) * rows]
                part = part.astype(f32) if m else activate(part)
                part = jnp.where(col_there[n], part, 0.0)
                put(stage, (m, down(2, (-NEAR, cols)[n] + c)), part)
    def corner_at(d, m, q):
        first = ((2 * d + m) * 2 + q) * NEAR
        return slice(first, first + NEAR)

    for n in range(2):
        for d in range(2):
            for m in range(2):
                for q in range(2):
                    h = (2 + d, rows + 1 - d)[n]
                    corner_f32[n, corner_at(d, m, q)] = take(stage, (m, near(h, q)))
        corner_out[n] = corner_f32[n].astype(bf16)
    for n in range(2):

        @pl.when(row_there[n])
        def _():
            corner_copy(n).start()

    send_row(later, 1, (1, 0))

    products(*halves[1])
    inner_rows(*halves[0])
    flip(k1, k1t)
    send_row(sooner, 1, (1, 0))
    def out_store(at, back):
        for t in range(step):
            put(outs, (pl.ds(at + t, TILE, stride=step),), back[t * TILE : (t + 1) * TILE])

    def finish(n):
        value = take(outs, (slice(n * cols, (n + 1) * cols),)) * gain[n]
        o_ref[0, n] = (value + xg[1, n].astype(f32)).astype(bf16)

    side_cols = (-1, 0, cols - 1, cols)

    def beside(m):
        return lambda i, j: [
            take(stage, (m, down(i + 1, col + j - 1))).astype(bf16) for col in side_cols
        ]

    value = inner_value(contract(k2t, every, [beside(1)]), contract(k1, every, [beside(0)]))
    inner_rows(*halves[1])
    for q, (col, there) in enumerate(zip(side_cols, (left, None, None, right))):
        part = value[q * TILE : q * TILE + rows]
        put(ins, (down(1, col),), part if there is None else jnp.where(there, part, 0.0))
    for n in range(2, rows):
        inner_tiles(ins, n, n)

    half = (rows - 4) // 2
    for place in (2, 2 + half):
        back = contract(k1t, every, [body(icat, place, half, 0, cols)])
        for q in range(half):
            out_store((place + q) * cols, back[q * cols : (q + 1) * cols])

    for n in range(2):

        @pl.when(row_there[n])
        def _():
            row_both(1 - n, 0).wait_recv()
            corner_copy(1 - n).wait_recv()

    def ends_at(h, j):
        return pl.ds(h * span + TILE + j - 2, 2, stride=cols + 1)

    def edge_tiles(n, h):
        for m in range(2):
            for j in range(3):
                place = h - n * rows
                edge_cat[n, m, place, j, :2] = take(stage, (m, ends_at(h, j)))

    def stage_halo(n):
        h = (1, rows + 2)[n]
        for m in range(2):
            value = row_halo[n, 0, m]
            value = value.astype(f32) if m else activate(value)
            put(stage, (m, inside(h)), jnp.where(row_there[n], value, 0.0))
            for q in range(2):
                put(stage, (m, near(h, q)), corner_f32[n, corner_at(0, m, q)])
            tiles(m, h, range(step + 2))
        edge_tiles(n, h)

    def line(n, m, place):
        def piece(i, j):
            ends = edge_cat[n, m, place + i - n * rows, j].astype(bf16)
            return [cat[m, place + i, j * TILE : j * TILE + cols], ends]

        return piece

    place_in = lax.broadcasted_iota(jnp.int32, (TILE, chans), 0)
    ends_ok = jnp.logical_or(
        jnp.logical_and(place_in == 0, left), jnp.logical_and(place_in == 1, right)
    )

    def edge_store(ref, row, place, value):
        main, ends = value[:cols], jnp.where(ends_ok, value[cols:], 0.0)
        inner_store(ref, row, main)
        for q, col in enumerate((-1, cols)):
            at = row * span + TILE + col
            put(ref, (slice(at, at + 1),), ends[q : q + 1])
        inner_tiles(ref, row, place)

    for n in range(2):
        corner_f32[n] = jnp.where(row_there[n], corner_in[n].astype(f32), 0.0)
        stage_halo(n)
        for h in ((2, 3), (rows, rows + 1))[n]:
            for m in range(2):
                tiles(m, h, (0, step + 1))
            edge_tiles(n, h)
    wide = cols + TILE
    places = ((0, 1), (rows + 1, rows))
    lines = [[line(n, m, place) for n in range(2) for place in places[n]] for m in range(2)]
    back = contract(k2t, every, lines[1])
    pre = contract(k1, every, lines[0])
    for n in range(2, rows - 2):
        finish(n)
    for n, (outer, place) in enumerate(places):
        first = 2 * n * wide
        back_part[n] = back[first : first + wide]
        pre_part[n] = pre[first : first + wide]
        first += wide
        edge_store(ins, place, place, inner_value(back[first : first + wide], pre[first : first + wide]))

    for n, place in enumerate((0, rows - 2)):
        back = contract(k1t, every, [body(icat, place, 2, 0, cols)])
        out_edge[n] = back[n * cols : (n + 1) * cols]
        inner = (1, rows - 2)[n]
        out_store(inner * cols, back[(1 - n) * cols : (2 - n) * cols])
        finish(inner)

    def last_rows(n):
        h, outer, place = n * (rows + 3), n * (rows + 1), n * (rows - 1)

        @pl.when(beyond(n))
        def _():
            row_both(1 - n, 1).wait_recv()
            for m in range(2):
                value = row_halo[n, 1, m]
                value = value.astype(f32) if m else activate(value)
                halo = far.at[n, m]
                put(halo, (inside(0),), value)
                for q in range(2):
                    put(halo, (near(0, q),), corner_f32[n, corner_at(1, m, q)])
                for t in range(step + 2):
                    part = take(halo, (pl.ds(TILE + t - 1, TILE, stride=step),))
                    cat[m, h, t * TILE : (t + 1) * TILE] = part.astype(bf16)
                for j in range(3):
                    edge_cat[n, m, 3 * n, j, :2] = take(halo, (ends_at(0, j),))

            def tap(weights, pieces):
                lhs = jnp.concatenate([jnp.concatenate(pieces(j), 0) for j in range(3)], 1)
                rhs = weights[2 * n].reshape(3 * chans, chans)
                return jnp.dot(lhs, rhs, preferred_element_type=f32)

            def ends_line(m):
                return lambda j: [
                    cat[m, h, j * TILE : j * TILE + cols],
                    edge_cat[n, m, 3 * n, j].astype(bf16),
                ]

            back = tap(k2t, ends_line(1)) + back_part[n]
            pre = tap(k1, ends_line(0)) + pre_part[n]
            edge_store(edge_ins.at[n], 0, outer, inner_value(back, pre))
            out_edge[n] += tap(k1t, lambda j: [icat[outer, j * TILE : j * TILE + cols]])

        back = out_edge[n]
        for t in range(step):
            at = pl.ds(t, TILE, stride=step)
            put(edge_outs.at[n], (at,), back[t * TILE : (t + 1) * TILE])
        value = take(edge_outs.at[n], (slice(0, cols),)) * gain[place]
        o_ref[0, place] = (value + xg[1, place].astype(f32)).astype(bf16)

    last_rows(sooner)
    last_rows(later)

    for n in range(2):

        @pl.when(row_there[n])
        def _():
            for d in range(2):
                row_both(n, d).wait_send()
            corner_copy(n).wait_send()

        @pl.when(col_there[n])
        def _():
            for m in range(2):
                col_copy(n, m).wait_send()


def hand_over(source, target, sem):
    copy = pltpu.make_async_copy(source, target, sem)
    copy.start()
    copy.wait()


def per_device(
    image_in,
    cotangent,
    first_kernel,
    first_bias,
    second_kernel,
    first_center,
    first_inverse,
    first_gain,
    first_shift,
    second_center,
    second_inverse,
    second_gain,
    second_shift,
):
    _, rows, cols, chans = image_in.shape
    groups = first_center.shape[0]
    span, step = cols + 2 * TILE, cols // TILE
    lanes = chans // LANES
    bf16, f32 = jnp.bfloat16, jnp.float32
    vec = lambda v: v.reshape(1, chans)
    result = pl.pallas_call(
        functools.partial(kernel, rows, cols, chans, groups),
        out_shape=jax.ShapeDtypeStruct(image_in.shape, bf16),
        in_specs=[pl.BlockSpec(memory_space=pltpu.HBM)] * 13,
        out_specs=pl.BlockSpec(memory_space=pltpu.VMEM),
        scratch_shapes=[
            pltpu.VMEM((2, rows, cols, chans), bf16),
            pltpu.VMEM((3, 3, chans, chans), bf16),
            pltpu.VMEM((3, 3, chans, chans), bf16),
            pltpu.VMEM((3, 3, chans, chans), bf16),
            pltpu.VMEM((3, 3, chans, chans), bf16),
            pltpu.VMEM((5, 1, chans), f32),
            pltpu.SMEM((4, groups), f32),
            pltpu.VMEM((4, 1, chans), f32),
            pltpu.VMEM((2, lanes, (rows + 4) * span, LANES), f32),
            pltpu.VMEM((2, 2, lanes, rows * TILE, LANES), f32),
            pltpu.VMEM((2, 2, lanes, span, LANES), f32),
            pltpu.VMEM((lanes, (rows + 2) * span, LANES), f32),
            pltpu.VMEM((2, lanes, span, LANES), f32),
            pltpu.VMEM((lanes, rows * cols, LANES), f32),
            pltpu.VMEM((2, lanes, cols, LANES), f32),
            pltpu.VMEM((rows, cols, chans), f32),
            pltpu.VMEM((2, rows + 4, (step + 2) * TILE, chans), bf16),
            pltpu.VMEM((2, 2, 4, 3, TILE, chans), f32),
            pltpu.VMEM((rows + 2, (step + 2) * TILE, chans), bf16),
            pltpu.VMEM((rows + 2, cols, chans), f32),
            pltpu.VMEM((rows + 2, cols, chans), f32),
            pltpu.VMEM((2, cols + TILE, chans), f32),
            pltpu.VMEM((2, cols + TILE, chans), f32),
            pltpu.VMEM((2, cols, chans), f32),
            pltpu.VMEM((2, 2, 2, cols, chans), bf16),
            pltpu.VMEM((2, 2, NEAR * rows, chans), bf16),
            pltpu.VMEM((2, 2, NEAR * rows, chans), bf16),
            pltpu.VMEM((2, TILE, chans), f32),
            pltpu.VMEM((2, TILE, chans), bf16),
            pltpu.VMEM((2, TILE, chans), bf16),
            pltpu.SemaphoreType.DMA((9,)),
            pltpu.SemaphoreType.DMA((2, 2)),
            pltpu.SemaphoreType.DMA((2, 2)),
            pltpu.SemaphoreType.DMA((2, 2)),
            pltpu.SemaphoreType.DMA((2, 2)),
            pltpu.SemaphoreType.DMA((2,)),
            pltpu.SemaphoreType.DMA((2,)),
        ],
        compiler_params=pltpu.CompilerParams(
            collective_id=0, has_side_effects=True, vmem_limit_bytes=40 << 20
        ),
    )(
        *(
            pltpu.with_memory_space_constraint(value, pltpu.HBM)
            for value in (
                image_in,
                cotangent,
                first_kernel,
                vec(first_bias),
                second_kernel,
                first_center,
                first_inverse,
                vec(first_gain),
                vec(first_shift),
                second_center,
                second_inverse,
                vec(second_gain),
                vec(second_shift),
            )
        )
    )
    return pl.pallas_call(
        hand_over,
        out_shape=jax.ShapeDtypeStruct(image_in.shape, bf16),
        in_specs=[pl.BlockSpec(memory_space=pltpu.VMEM)],
        out_specs=pl.BlockSpec(memory_space=pltpu.HBM),
        scratch_shapes=[pltpu.SemaphoreType.DMA],
        compiler_params=pltpu.CompilerParams(vmem_limit_bytes=8 << 20),
    )(result)


def solution(mesh):
    return jax.shard_map(
        per_device,
        mesh=mesh,
        in_specs=(P(None, "rows", "cols", None),) * 2 + (P(),) * 11,
        out_specs=P(None, "rows", "cols", None),
        check_vma=False,
    )
```

```python
import functools

import jax
import jax.numpy as jnp
from jax import lax
from jax.experimental import pallas as pl
from jax.experimental.pallas import tpu as pltpu
from jax.sharding import PartitionSpec as P

MESH = pl.DeviceIdType.MESH
TILE = 16
LANES = 128
NEAR = 2
SIDES = (-1, 1)


def kernel(
    rows,
    cols,
    chans,
    groups,
    x_hbm,
    g_hbm,
    k1_hbm,
    b1_hbm,
    k2_hbm,
    c1_hbm,
    v1_hbm,
    n1_hbm,
    s1_hbm,
    c2_hbm,
    v2_hbm,
    n2_hbm,
    s2_hbm,
    o_ref,
    k1,
    k2t,
    k1t,
    params,
    gain,
    xg,
    back_part,
    pre_part,
    out_edge,
    corner_f32,
    last_halo,
    k2,
    vecs,
    scal,
    stage,
    raw,
    far,
    ins,
    edge_ins,
    outs,
    edge_outs,
    cat,
    edge_cat,
    icat,
    back_main,
    pre_main,
    row_halo,
    pack,
    col_halo,
    corner_out,
    corner_in,
    load_sem,
    row_send,
    row_recv,
    col_send,
    col_recv,
    corner_send,
    corner_recv,
):
    span = cols + 2 * TILE
    step = cols // TILE
    lane_parts = [slice(k, k + LANES) for k in range(0, chans, LANES)]
    f32, bf16 = jnp.float32, jnp.bfloat16
    my_row, my_col = lax.axis_index("rows"), lax.axis_index("cols")
    n_rows, n_cols = lax.axis_size("rows"), lax.axis_size("cols")
    above, below = my_row > 0, my_row < n_rows - 1
    left, right = my_col > 0, my_col < n_cols - 1
    row_there, col_there = (above, below), (left, right)

    barrier = pltpu.get_barrier_semaphore()
    for n, side in enumerate(SIDES):

        @pl.when(col_there[n])
        def _():
            pl.semaphore_signal(
                barrier, inc=1, device_id=(my_row, my_col + side), device_id_type=MESH
            )

        @pl.when(row_there[n])
        def _():
            pl.semaphore_signal(
                barrier, inc=1, device_id=(my_row + side, my_col), device_id_type=MESH
            )

    load_k2 = pltpu.make_async_copy(k2_hbm, k2, load_sem.at[0])
    load_k1 = pltpu.make_async_copy(k1_hbm, k1, load_sem.at[1])
    load_x = pltpu.make_async_copy(x_hbm.at[0], xg.at[0], load_sem.at[2])
    load_g = pltpu.make_async_copy(g_hbm.at[0], xg.at[1], load_sem.at[3])
    load_g.start()
    load_x.start()
    for n, ref in enumerate((b1_hbm, n1_hbm, s1_hbm, n2_hbm, s2_hbm)):
        pltpu.make_async_copy(ref, vecs.at[n], load_sem.at[4]).start()
    for n, ref in enumerate((c1_hbm, v1_hbm, c2_hbm, v2_hbm)):
        pltpu.make_async_copy(ref, scal.at[n], load_sem.at[5 + n]).start()
    load_k2.start()
    load_k1.start()

    def one(there):
        return jnp.where(there, 1, 0)


    def row_link(n, d, src, dst):
        return pltpu.make_async_remote_copy(
            src_ref=src,
            dst_ref=dst,
            send_sem=row_send.at[n, d],
            recv_sem=row_recv.at[1 - n, d],
            device_id=(my_row + 2 * n - 1, my_col),
            device_id_type=MESH,
        )

    def beyond(n):
        return jnp.logical_and(my_row + 2 * n >= 1, my_row + 2 * n < n_rows + 1)

    def send_row(n, d, which):
        @pl.when(beyond(n))
        def _():
            for m in which:
                src = (x_hbm, g_hbm)[m].at[0, d + n * (rows - 1 - 2 * d)]
                row_link(n, d, src, row_halo.at[1 - n, d, m]).start()

    sooner = my_row % 2
    later = 1 - sooner

    def row_both(n, d):
        return row_link(n, d, row_halo.at[1 - n, d], row_halo.at[1 - n, d])

    def col_copy(n, m):
        return pltpu.make_async_remote_copy(
            src_ref=pack.at[n, m],
            dst_ref=col_halo.at[1 - n, m],
            send_sem=col_send.at[n, m],
            recv_sem=col_recv.at[1 - n, m],
            device_id=(my_row, my_col + SIDES[n]),
            device_id_type=MESH,
        )

    def corner_copy(n):
        return pltpu.make_async_remote_copy(
            src_ref=corner_out.at[n],
            dst_ref=corner_in.at[1 - n],
            send_sem=corner_send.at[n],
            recv_sem=corner_recv.at[1 - n],
            device_id=(my_row + SIDES[n], my_col),
            device_id_type=MESH,
        )


    def flip(source, target):
        for i in range(3):
            for j in range(3):
                target[i, j] = source[2 - i, 2 - j].T

    def put(ref, at, value):
        for k, lanes in enumerate(lane_parts):
            ref[(*at[:-1], k, at[-1])] = value[:, lanes]

    def take(ref, at):
        return jnp.concatenate([ref[(*at[:-1], k, at[-1])] for k in range(len(lane_parts))], 1)

    def near(h, n):
        first = h * span + (TILE - NEAR, TILE + cols)[n]
        return slice(first, first + NEAR)

    def inside(h):
        return slice(h * span + TILE, h * span + TILE + cols)

    def down(h, col):
        return pl.ds(h * span + TILE + col, rows, stride=span)

    def tiles(m, h, which):
        for t in which:
            part = take(stage, (m, pl.ds(h * span + TILE + t - 1, TILE, stride=step)))
            cat[m, h, t * TILE : (t + 1) * TILE] = part.astype(bf16)

    def pack_cols(m):
        for n in range(2):
            for r in range(rows):
                tile = xg[m, r, (0, cols - TILE)[n] : (TILE, cols)[n]].astype(f32)
                put(raw, (n, m, slice(r * TILE, (r + 1) * TILE)), tile)
            for c in range(NEAR):
                column = pl.ds((0, TILE - NEAR)[n] + c, rows, stride=TILE)
                part = take(raw, (n, m, column))
                pack[n, m, c * rows : (c + 1) * rows] = part.astype(bf16)

    def send_cols(m):
        for n in range(2):

            @pl.when(col_there[n])
            def _():
                col_copy(n, m).start()

    for h in (0, rows + 1):
        icat[h] = jnp.zeros(icat.shape[1:], bf16)
    for h in (0, rows + 3):
        for m in range(2):
            cat[m, h] = jnp.zeros(cat.shape[2:], bf16)
    edge_cat[...] = jnp.zeros(edge_cat.shape, f32)

    load_g.wait()
    for n in range(rows):
        put(stage, (1, inside(n + 2)), xg[1, n].astype(f32))
    pack_cols(1)
    pltpu.make_async_copy(vecs, vecs, load_sem.at[4]).wait()
    for n, ref in enumerate((c1_hbm, v1_hbm, c2_hbm, v2_hbm)):
        pltpu.make_async_copy(ref, scal.at[n], load_sem.at[5 + n]).wait()
    lane_group = lax.broadcasted_iota(jnp.int32, (1, chans), 1) // (chans // groups)

    def spread(n):
        total = jnp.zeros((1, chans), f32)
        for q in range(groups):
            total = jnp.where(lane_group == q, scal[n, q], total)
        return total

    scale1 = spread(1) * vecs[1]
    scale2 = spread(3) * vecs[3]
    params[0] = 0.5 * scale1
    params[1] = 0.5 * (vecs[2] - spread(0) * scale1)
    params[2] = 0.5 * scale2
    params[3] = 0.5 * ((vecs[0] - spread(2)) * scale2 + vecs[4])

    pl.semaphore_wait(barrier, one(above) + one(below) + one(left) + one(right))
    for n in range(2):
        send_row(n, 0, (1,))
    send_cols(1)
    load_x.wait()
    pack_cols(0)
    send_cols(0)
    for n in range(2):
        send_row(n, 0, (0,))

    def activate(value):
        half_pre = value.astype(f32) * params[0] + params[1]
        return half_pre * (1.0 + jnp.tanh(half_pre))

    for n in range(rows):
        half_pre = xg[0, n].astype(f32) * params[0] + params[1]
        more = 1.0 + jnp.tanh(half_pre)
        act = half_pre * more
        put(stage, (0, inside(n + 2)), act)
        gain[n] = (1.0 + half_pre + half_pre - act) * (more * params[0])

    def slope(half_pre, factor):
        tanh = jnp.tanh(half_pre)
        return (1.0 + half_pre * (1.0 - tanh)) * ((1.0 + tanh) * factor)

    def inner_value(back, pre):
        return slope(pre * params[2] + params[3], back * params[2])

    every = (0, 1, 2)

    def contract(weights, taps, pieces):
        lhs = []
        for i in taps:
            for j in range(3):
                stack = [part for piece in pieces for part in piece(i, j)]
                lhs.append(stack[0] if len(stack) == 1 else jnp.concatenate(stack, 0))
        rhs = weights[taps[0] : taps[-1] + 1].reshape(len(taps) * 3 * chans, chans)
        return jnp.dot(jnp.concatenate(lhs, 1), rhs, preferred_element_type=f32)

    def body(ref, place, count, start, width):
        def piece(i, j):
            part = ref[place + i : place + i + count, (start + j) * TILE : (start + j) * TILE + width]
            return [part.reshape(count * width, chans)]

        return piece

    half = rows // 2
    halves = ((2, half), (2 + half, rows - 2 - half))

    def inner_store(ref, n, value):
        for t in range(step):
            at = pl.ds(n * span + TILE + t, TILE, stride=step)
            put(ref, (at,), value[t * TILE : (t + 1) * TILE])

    def inner_tiles(ref, n, h):
        for t in range(step + 2):
            part = take(ref, (pl.ds(n * span + TILE + t - 1, TILE, stride=step),))
            icat[h, t * TILE : (t + 1) * TILE] = part.astype(bf16)

    def products(place, count):
        back = contract(k2t, every, [body(cat.at[1], place, count, 0, cols)])
        pre = contract(k1, every, [body(cat.at[0], place, count, 0, cols)])
        for n in range(count):
            back_main[place + n] = back[n * cols : (n + 1) * cols]
            pre_main[place + n] = pre[n * cols : (n + 1) * cols]

    def inner_rows(place, count):
        for n in range(place, place + count):
            inner_store(ins, n, inner_value(back_main[n], pre_main[n]))

    load_k2.wait()
    load_k1.wait()
    flip(k2, k2t)
    for h in range(2, rows + 2):
        for m in range(2):
            tiles(m, h, range(step + 2))
    products(*halves[0])

    for m in (1, 0):
        for n in range(2):

            @pl.when(col_there[n])
            def _():
                col_copy(1 - n, m).wait_recv()

    for m in range(2):
        for n in range(2):
            for c in range(NEAR):
                part = col_halo[n, m, c * rows : (c + 1) * rows]
                part = part.astype(f32) if m else activate(part)
                part = jnp.where(col_there[n], part, 0.0)
                put(stage, (m, down(2, (-NEAR, cols)[n] + c)), part)
    def corner_at(d, m, q):
        first = ((2 * d + m) * 2 + q) * NEAR
        return slice(first, first + NEAR)

    for n in range(2):
        for d in range(2):
            for m in range(2):
                for q in range(2):
                    h = (2 + d, rows + 1 - d)[n]
                    corner_f32[n, corner_at(d, m, q)] = take(stage, (m, near(h, q)))
        corner_out[n] = corner_f32[n].astype(bf16)
    for n in range(2):

        @pl.when(row_there[n])
        def _():
            corner_copy(n).start()

    send_row(later, 1, (1, 0))

    products(*halves[1])
    inner_rows(*halves[0])
    flip(k1, k1t)
    send_row(sooner, 1, (1, 0))
    def out_store(at, back):
        for t in range(step):
            put(outs, (pl.ds(at + t, TILE, stride=step),), back[t * TILE : (t + 1) * TILE])

    def finish(n):
        value = take(outs, (slice(n * cols, (n + 1) * cols),)) * gain[n]
        o_ref[0, n] = (value + xg[1, n].astype(f32)).astype(bf16)

    side_cols = (-1, 0, cols - 1, cols)

    def beside(m):
        return lambda i, j: [
            take(stage, (m, down(i + 1, col + j - 1))).astype(bf16) for col in side_cols
        ]

    value = inner_value(contract(k2t, every, [beside(1)]), contract(k1, every, [beside(0)]))
    inner_rows(*halves[1])
    for q, (col, there) in enumerate(zip(side_cols, (left, None, None, right))):
        part = value[q * TILE : q * TILE + rows]
        put(ins, (down(1, col),), part if there is None else jnp.where(there, part, 0.0))
    for n in range(2, rows):
        inner_tiles(ins, n, n)

    half = (rows - 4) // 2
    for place in (2, 2 + half):
        back = contract(k1t, every, [body(icat, place, half, 0, cols)])
        for q in range(half):
            out_store((place + q) * cols, back[q * cols : (q + 1) * cols])

    for n in range(2):

        @pl.when(row_there[n])
        def _():
            row_both(1 - n, 0).wait_recv()
            corner_copy(1 - n).wait_recv()

    def ends_at(h, j):
        return pl.ds(h * span + TILE + j - 2, 2, stride=cols + 1)

    def edge_tiles(n, h):
        for m in range(2):
            for j in range(3):
                place = h - n * rows
                edge_cat[n, m, place, j, :2] = take(stage, (m, ends_at(h, j)))

    def stage_halo(n):
        h = (1, rows + 2)[n]
        for m in range(2):
            value = row_halo[n, 0, m]
            value = value.astype(f32) if m else activate(value)
            put(stage, (m, inside(h)), jnp.where(row_there[n], value, 0.0))
            for q in range(2):
                put(stage, (m, near(h, q)), corner_f32[n, corner_at(0, m, q)])
            tiles(m, h, range(step + 2))
        edge_tiles(n, h)

    def line(n, m, place):
        def piece(i, j):
            ends = edge_cat[n, m, place + i - n * rows, j].astype(bf16)
            return [cat[m, place + i, j * TILE : j * TILE + cols], ends]

        return piece

    place_in = lax.broadcasted_iota(jnp.int32, (TILE, chans), 0)
    ends_ok = jnp.logical_or(
        jnp.logical_and(place_in == 0, left), jnp.logical_and(place_in == 1, right)
    )

    def edge_store(ref, row, place, value):
        main, ends = value[:cols], jnp.where(ends_ok, value[cols:], 0.0)
        inner_store(ref, row, main)
        for q, col in enumerate((-1, cols)):
            at = row * span + TILE + col
            put(ref, (slice(at, at + 1),), ends[q : q + 1])
        inner_tiles(ref, row, place)

    for n in range(2):
        corner_f32[n] = jnp.where(row_there[n], corner_in[n].astype(f32), 0.0)
        stage_halo(n)
        for h in ((2, 3), (rows, rows + 1))[n]:
            for m in range(2):
                tiles(m, h, (0, step + 1))
            edge_tiles(n, h)
    wide = cols + TILE
    places = ((0, 1), (rows + 1, rows))
    lines = [[line(n, m, place) for n in range(2) for place in places[n]] for m in range(2)]
    back = contract(k2t, every, lines[1])
    pre = contract(k1, every, lines[0])
    for n in range(2, rows - 2):
        finish(n)
    for n, (outer, place) in enumerate(places):
        first = 2 * n * wide
        back_part[n] = back[first : first + wide]
        pre_part[n] = pre[first : first + wide]
        first += wide
        edge_store(ins, place, place, inner_value(back[first : first + wide], pre[first : first + wide]))

    for n, place in enumerate((0, rows - 2)):
        back = contract(k1t, every, [body(icat, place, 2, 0, cols)])
        out_edge[n] = back[n * cols : (n + 1) * cols]
        inner = (1, rows - 2)[n]
        out_store(inner * cols, back[(1 - n) * cols : (2 - n) * cols])
        finish(inner)

    def last_rows(n):
        h, outer, place = n * (rows + 3), n * (rows + 1), n * (rows - 1)

        @pl.when(beyond(n))
        def _():
            row_both(1 - n, 1).wait_recv()
            for m in range(2):
                value = row_halo[n, 1, m]
                value = value.astype(f32) if m else activate(value)
                halo = far.at[n, m]
                put(halo, (inside(0),), value)
                for q in range(2):
                    put(halo, (near(0, q),), corner_f32[n, corner_at(1, m, q)])
                for t in range(step + 2):
                    part = take(halo, (pl.ds(TILE + t - 1, TILE, stride=step),))
                    cat[m, h, t * TILE : (t + 1) * TILE] = part.astype(bf16)
                for j in range(3):
                    edge_cat[n, m, 3 * n, j, :2] = take(halo, (ends_at(0, j),))

            def tap(weights, pieces):
                lhs = jnp.concatenate([jnp.concatenate(pieces(j), 0) for j in range(3)], 1)
                rhs = weights[2 * n].reshape(3 * chans, chans)
                return jnp.dot(lhs, rhs, preferred_element_type=f32)

            def ends_line(m):
                return lambda j: [
                    cat[m, h, j * TILE : j * TILE + cols],
                    edge_cat[n, m, 3 * n, j].astype(bf16),
                ]

            back = tap(k2t, ends_line(1)) + back_part[n]
            pre = tap(k1, ends_line(0)) + pre_part[n]
            edge_store(edge_ins.at[n], 0, outer, inner_value(back, pre))
            out_edge[n] += tap(k1t, lambda j: [icat[outer, j * TILE : j * TILE + cols]])

        back = out_edge[n]
        for t in range(step):
            at = pl.ds(t, TILE, stride=step)
            put(edge_outs.at[n], (at,), back[t * TILE : (t + 1) * TILE])
        value = take(edge_outs.at[n], (slice(0, cols),)) * gain[place]
        o_ref[0, place] = (value + xg[1, place].astype(f32)).astype(bf16)

    last_rows(sooner)
    @pl.when(beyond(later))
    def _():
        row_both(1 - later, 1).wait_recv()
        last_halo[...] = row_halo[later, 1]

    for n in range(2):

        @pl.when(row_there[n])
        def _():
            for d in range(2):
                row_both(n, d).wait_send()
            corner_copy(n).wait_send()

        @pl.when(col_there[n])
        def _():
            for m in range(2):
                col_copy(n, m).wait_send()


def hand_over(
    rows,
    cols,
    chans,
    o_in,
    k1,
    k2t,
    k1t,
    params,
    gain,
    xg,
    back_part,
    pre_part,
    out_edge,
    corner_f32,
    last_halo,
    target,
    stage,
    ins,
    cat,
    edge_cat,
    icat,
    outs,
    total,
    last,
    sem,
):
    span, step = cols + 2 * TILE, cols // TILE
    lane_parts = [slice(k, k + LANES) for k in range(0, chans, LANES)]
    f32, bf16 = jnp.float32, jnp.bfloat16
    my_row, n_rows = lax.axis_index("rows"), lax.axis_size("rows")
    my_col, n_cols = lax.axis_index("cols"), lax.axis_size("cols")
    n = 1 - my_row % 2
    place = n * (rows - 1)
    most = pl.ds(1 - n, rows - 1)
    early = pltpu.make_async_copy(o_in.at[0, most], target.at[0, most], sem.at[0])
    early.start()

    def put(ref, at, value):
        for k, lanes in enumerate(lane_parts):
            ref[k, at] = value[:, lanes]

    def take(ref, at):
        return jnp.concatenate([ref[k, at] for k in range(len(lane_parts))], 1)

    def tap(weights, pieces):
        lhs = jnp.concatenate([jnp.concatenate(pieces(j), 0) for j in range(3)], 1)
        rhs = weights[2 * n].reshape(3 * chans, chans)
        return jnp.dot(lhs, rhs, preferred_element_type=f32)

    total[...] = out_edge[n]
    there = jnp.logical_and(my_row + 2 * n >= 1, my_row + 2 * n < n_rows + 1)

    @pl.when(there)
    def _():
        for m in range(2):
            value = last_halo[m].astype(f32)
            if m == 0:
                value = value * params[0] + params[1]
                value = value * (1.0 + jnp.tanh(value))
            halo = stage.at[m]
            put(halo, slice(TILE, TILE + cols), value)
            for q, at in enumerate((TILE - NEAR, TILE + cols)):
                first = ((2 + m) * 2 + q) * NEAR
                put(halo, slice(at, at + NEAR), corner_f32[n, first : first + NEAR])
            for t in range(step + 2):
                part = take(halo, pl.ds(TILE + t - 1, TILE, stride=step))
                cat[m, t * TILE : (t + 1) * TILE] = part.astype(bf16)
            for j in range(3):
                ends = pl.ds(TILE + j - 2, 2, stride=cols + 1)
                edge_cat[m, j] = jnp.zeros((TILE, chans), f32)
                edge_cat[m, j, :2] = take(halo, ends)

        def line(m):
            return lambda j: [
                cat[m, j * TILE : j * TILE + cols],
                edge_cat[m, j].astype(bf16),
            ]

        back = (tap(k2t, line(1)) + back_part[n]) * params[2]
        pre = (tap(k1, line(0)) + pre_part[n]) * params[2] + params[3]
        tanh = jnp.tanh(pre)
        value = (1.0 + pre * (1.0 - tanh)) * ((1.0 + tanh) * back)
        for t in range(step):
            at = pl.ds(TILE + t, TILE, stride=step)
            put(ins, at, value[t * TILE : (t + 1) * TILE])
        for q, (at, ok) in enumerate(((TILE - 1, my_col > 0), (TILE + cols, my_col < n_cols - 1))):
            put(ins, slice(at, at + 1), jnp.where(ok, value[cols + q : cols + q + 1], 0.0))
        for t in range(step + 2):
            part = take(ins, pl.ds(TILE + t - 1, TILE, stride=step))
            icat[t * TILE : (t + 1) * TILE] = part.astype(bf16)
        total[...] += tap(k1t, lambda j: [icat[j * TILE : j * TILE + cols]])

    for t in range(step):
        put(outs, pl.ds(t, TILE, stride=step), total[t * TILE : (t + 1) * TILE])
    value = take(outs, slice(0, cols)) * gain[place] + xg[1, place].astype(f32)
    last[...] = value.astype(bf16)
    late = pltpu.make_async_copy(last, target.at[0, place], sem.at[1])
    late.start()
    early.wait()
    late.wait()


def per_device(
    image_in,
    cotangent,
    first_kernel,
    first_bias,
    second_kernel,
    first_center,
    first_inverse,
    first_gain,
    first_shift,
    second_center,
    second_inverse,
    second_gain,
    second_shift,
):
    _, rows, cols, chans = image_in.shape
    groups = first_center.shape[0]
    span, step = cols + 2 * TILE, cols // TILE
    lanes = chans // LANES
    bf16, f32 = jnp.bfloat16, jnp.float32
    vec = lambda v: v.reshape(1, chans)
    result = pl.pallas_call(
        functools.partial(kernel, rows, cols, chans, groups),
        out_shape=(
            jax.ShapeDtypeStruct(image_in.shape, bf16),
            jax.ShapeDtypeStruct((3, 3, chans, chans), bf16),
            jax.ShapeDtypeStruct((3, 3, chans, chans), bf16),
            jax.ShapeDtypeStruct((3, 3, chans, chans), bf16),
            jax.ShapeDtypeStruct((4, 1, chans), f32),
            jax.ShapeDtypeStruct((rows, cols, chans), f32),
            jax.ShapeDtypeStruct((2, rows, cols, chans), bf16),
            jax.ShapeDtypeStruct((2, cols + TILE, chans), f32),
            jax.ShapeDtypeStruct((2, cols + TILE, chans), f32),
            jax.ShapeDtypeStruct((2, cols, chans), f32),
            jax.ShapeDtypeStruct((2, TILE, chans), f32),
            jax.ShapeDtypeStruct((2, cols, chans), bf16),
        ),
        in_specs=[pl.BlockSpec(memory_space=pltpu.HBM)] * 13,
        out_specs=(pl.BlockSpec(memory_space=pltpu.VMEM),) * 12,
        scratch_shapes=[
            pltpu.VMEM((3, 3, chans, chans), bf16),
            pltpu.VMEM((5, 1, chans), f32),
            pltpu.SMEM((4, groups), f32),
            pltpu.VMEM((2, lanes, (rows + 4) * span, LANES), f32),
            pltpu.VMEM((2, 2, lanes, rows * TILE, LANES), f32),
            pltpu.VMEM((2, 2, lanes, span, LANES), f32),
            pltpu.VMEM((lanes, (rows + 2) * span, LANES), f32),
            pltpu.VMEM((2, lanes, span, LANES), f32),
            pltpu.VMEM((lanes, rows * cols, LANES), f32),
            pltpu.VMEM((2, lanes, cols, LANES), f32),
            pltpu.VMEM((2, rows + 4, (step + 2) * TILE, chans), bf16),
            pltpu.VMEM((2, 2, 4, 3, TILE, chans), f32),
            pltpu.VMEM((rows + 2, (step + 2) * TILE, chans), bf16),
            pltpu.VMEM((rows + 2, cols, chans), f32),
            pltpu.VMEM((rows + 2, cols, chans), f32),
            pltpu.VMEM((2, 2, 2, cols, chans), bf16),
            pltpu.VMEM((2, 2, NEAR * rows, chans), bf16),
            pltpu.VMEM((2, 2, NEAR * rows, chans), bf16),
            pltpu.VMEM((2, TILE, chans), bf16),
            pltpu.VMEM((2, TILE, chans), bf16),
            pltpu.SemaphoreType.DMA((9,)),
            pltpu.SemaphoreType.DMA((2, 2)),
            pltpu.SemaphoreType.DMA((2, 2)),
            pltpu.SemaphoreType.DMA((2, 2)),
            pltpu.SemaphoreType.DMA((2, 2)),
            pltpu.SemaphoreType.DMA((2,)),
            pltpu.SemaphoreType.DMA((2,)),
        ],
        compiler_params=pltpu.CompilerParams(
            collective_id=0, has_side_effects=True, vmem_limit_bytes=40 << 20
        ),
    )(
        *(
            pltpu.with_memory_space_constraint(value, pltpu.HBM)
            for value in (
                image_in,
                cotangent,
                first_kernel,
                vec(first_bias),
                second_kernel,
                first_center,
                first_inverse,
                vec(first_gain),
                vec(first_shift),
                second_center,
                second_inverse,
                vec(second_gain),
                vec(second_shift),
            )
        )
    )
    return pl.pallas_call(
        functools.partial(hand_over, rows, cols, chans),
        out_shape=jax.ShapeDtypeStruct(image_in.shape, bf16),
        in_specs=[pl.BlockSpec(memory_space=pltpu.VMEM)] * len(result),
        out_specs=pl.BlockSpec(memory_space=pltpu.HBM),
        scratch_shapes=[
            pltpu.VMEM((2, lanes, span, LANES), f32),
            pltpu.VMEM((lanes, span, LANES), f32),
            pltpu.VMEM((2, (step + 2) * TILE, chans), bf16),
            pltpu.VMEM((2, 3, TILE, chans), f32),
            pltpu.VMEM(((step + 2) * TILE, chans), bf16),
            pltpu.VMEM((lanes, cols, LANES), f32),
            pltpu.VMEM((cols, chans), f32),
            pltpu.VMEM((cols, chans), bf16),
            pltpu.SemaphoreType.DMA((2,)),
        ],
        compiler_params=pltpu.CompilerParams(vmem_limit_bytes=8 << 20),
    )(*result)


def solution(mesh):
    return jax.shard_map(
        per_device,
        mesh=mesh,
        in_specs=(P(None, "rows", "cols", None),) * 2 + (P(),) * 11,
        out_specs=P(None, "rows", "cols", None),
        check_vma=False,
    )
```

```python
import functools

import jax
import jax.numpy as jnp
from jax import lax
from jax.experimental import pallas as pl
from jax.experimental.pallas import tpu as pltpu
from jax.sharding import PartitionSpec as P

MESH = pl.DeviceIdType.MESH
TILE = 16
LANES = 128
NEAR = 2
SIDES = (-1, 1)


def kernel(
    rows,
    cols,
    chans,
    groups,
    x_hbm,
    g_hbm,
    k1_hbm,
    b1_hbm,
    k2_hbm,
    c1_hbm,
    v1_hbm,
    n1_hbm,
    s1_hbm,
    c2_hbm,
    v2_hbm,
    n2_hbm,
    s2_hbm,
    o_ref,
    k1,
    k2t,
    k1t,
    params,
    gain,
    xg,
    back_part,
    pre_part,
    out_edge,
    corner_f32,
    last_halo,
    k2,
    vecs,
    scal,
    stage,
    raw,
    far,
    ins,
    edge_ins,
    outs,
    edge_outs,
    cat,
    edge_cat,
    icat,
    back_main,
    pre_main,
    row_halo,
    pack,
    col_halo,
    corner_out,
    corner_in,
    load_sem,
    row_send,
    row_recv,
    col_send,
    col_recv,
    corner_send,
    corner_recv,
):
    span = cols + 2 * TILE
    step = cols // TILE
    lane_parts = [slice(k, k + LANES) for k in range(0, chans, LANES)]
    f32, bf16 = jnp.float32, jnp.bfloat16
    my_row, my_col = lax.axis_index("rows"), lax.axis_index("cols")
    n_rows, n_cols = lax.axis_size("rows"), lax.axis_size("cols")
    above, below = my_row > 0, my_row < n_rows - 1
    left, right = my_col > 0, my_col < n_cols - 1
    row_there, col_there = (above, below), (left, right)

    barrier = pltpu.get_barrier_semaphore()
    for n, side in enumerate(SIDES):

        @pl.when(col_there[n])
        def _():
            pl.semaphore_signal(
                barrier, inc=1, device_id=(my_row, my_col + side), device_id_type=MESH
            )

        @pl.when(row_there[n])
        def _():
            pl.semaphore_signal(
                barrier, inc=1, device_id=(my_row + side, my_col), device_id_type=MESH
            )

    load_k2 = pltpu.make_async_copy(k2_hbm, k2, load_sem.at[0])
    load_k1 = pltpu.make_async_copy(k1_hbm, k1, load_sem.at[1])
    load_x = pltpu.make_async_copy(x_hbm.at[0], xg.at[0], load_sem.at[2])
    load_g = pltpu.make_async_copy(g_hbm.at[0], xg.at[1], load_sem.at[3])
    load_g.start()
    load_x.start()
    for n, ref in enumerate((b1_hbm, n1_hbm, s1_hbm, n2_hbm, s2_hbm)):
        pltpu.make_async_copy(ref, vecs.at[n], load_sem.at[4]).start()
    for n, ref in enumerate((c1_hbm, v1_hbm, c2_hbm, v2_hbm)):
        pltpu.make_async_copy(ref, scal.at[n], load_sem.at[5 + n]).start()
    load_k2.start()
    load_k1.start()

    def one(there):
        return jnp.where(there, 1, 0)


    def row_link(n, d, src, dst):
        return pltpu.make_async_remote_copy(
            src_ref=src,
            dst_ref=dst,
            send_sem=row_send.at[n, d],
            recv_sem=row_recv.at[1 - n, d],
            device_id=(my_row + 2 * n - 1, my_col),
            device_id_type=MESH,
        )

    def beyond(n):
        return jnp.logical_and(my_row + 2 * n >= 1, my_row + 2 * n < n_rows + 1)

    def send_row(n, d, which):
        @pl.when(beyond(n))
        def _():
            for m in which:
                src = (x_hbm, g_hbm)[m].at[0, d + n * (rows - 1 - 2 * d)]
                row_link(n, d, src, row_halo.at[1 - n, d, m]).start()

    sooner = my_row % 2
    later = 1 - sooner

    def row_both(n, d):
        return row_link(n, d, row_halo.at[1 - n, d], row_halo.at[1 - n, d])

    def col_copy(n, m):
        return pltpu.make_async_remote_copy(
            src_ref=pack.at[n, m],
            dst_ref=col_halo.at[1 - n, m],
            send_sem=col_send.at[n, m],
            recv_sem=col_recv.at[1 - n, m],
            device_id=(my_row, my_col + SIDES[n]),
            device_id_type=MESH,
        )

    def corner_copy(n):
        return pltpu.make_async_remote_copy(
            src_ref=corner_out.at[n],
            dst_ref=corner_in.at[1 - n],
            send_sem=corner_send.at[n],
            recv_sem=corner_recv.at[1 - n],
            device_id=(my_row + SIDES[n], my_col),
            device_id_type=MESH,
        )


    def flip(source, target):
        for i in range(3):
            for j in range(3):
                target[i, j] = source[2 - i, 2 - j].T

    def put(ref, at, value):
        for k, lanes in enumerate(lane_parts):
            ref[(*at[:-1], k, at[-1])] = value[:, lanes]

    def take(ref, at):
        return jnp.concatenate([ref[(*at[:-1], k, at[-1])] for k in range(len(lane_parts))], 1)

    def near(h, n):
        first = h * span + (TILE - NEAR, TILE + cols)[n]
        return slice(first, first + NEAR)

    def inside(h):
        return slice(h * span + TILE, h * span + TILE + cols)

    def down(h, col):
        return pl.ds(h * span + TILE + col, rows, stride=span)

    def tiles(m, h, which):
        for t in which:
            part = take(stage, (m, pl.ds(h * span + TILE + t - 1, TILE, stride=step)))
            cat[m, h, t * TILE : (t + 1) * TILE] = part.astype(bf16)

    def pack_cols(m):
        for n in range(2):
            for r in range(rows):
                tile = xg[m, r, (0, cols - TILE)[n] : (TILE, cols)[n]].astype(f32)
                put(raw, (n, m, slice(r * TILE, (r + 1) * TILE)), tile)
            for c in range(NEAR):
                column = pl.ds((0, TILE - NEAR)[n] + c, rows, stride=TILE)
                part = take(raw, (n, m, column))
                pack[n, m, c * rows : (c + 1) * rows] = part.astype(bf16)

    def send_cols(m):
        for n in range(2):

            @pl.when(col_there[n])
            def _():
                col_copy(n, m).start()

    for h in (0, rows + 1):
        icat[h] = jnp.zeros(icat.shape[1:], bf16)
    for h in (0, rows + 3):
        for m in range(2):
            cat[m, h] = jnp.zeros(cat.shape[2:], bf16)
    edge_cat[...] = jnp.zeros(edge_cat.shape, f32)

    load_g.wait()
    for n in range(rows):
        put(stage, (1, inside(n + 2)), xg[1, n].astype(f32))
    pack_cols(1)
    pltpu.make_async_copy(vecs, vecs, load_sem.at[4]).wait()
    for n, ref in enumerate((c1_hbm, v1_hbm, c2_hbm, v2_hbm)):
        pltpu.make_async_copy(ref, scal.at[n], load_sem.at[5 + n]).wait()
    lane_group = lax.broadcasted_iota(jnp.int32, (1, chans), 1) // (chans // groups)

    def spread(n):
        total = jnp.zeros((1, chans), f32)
        for q in range(groups):
            total = jnp.where(lane_group == q, scal[n, q], total)
        return total

    scale1 = spread(1) * vecs[1]
    scale2 = spread(3) * vecs[3]
    params[0] = 0.5 * scale1
    params[1] = 0.5 * (vecs[2] - spread(0) * scale1)
    params[2] = 0.5 * scale2
    params[3] = 0.5 * ((vecs[0] - spread(2)) * scale2 + vecs[4])

    pl.semaphore_wait(barrier, one(above) + one(below) + one(left) + one(right))
    for n in range(2):
        send_row(n, 0, (1,))
    send_cols(1)
    load_x.wait()
    pack_cols(0)
    send_cols(0)
    for n in range(2):
        send_row(n, 0, (0,))

    def activate(value):
        half_pre = value.astype(f32) * params[0] + params[1]
        return half_pre * (1.0 + jnp.tanh(half_pre))

    for n in range(rows):
        half_pre = xg[0, n].astype(f32) * params[0] + params[1]
        more = 1.0 + jnp.tanh(half_pre)
        act = half_pre * more
        put(stage, (0, inside(n + 2)), act)
        gain[n] = (1.0 + half_pre + half_pre - act) * (more * params[0])

    def slope(half_pre, factor):
        tanh = jnp.tanh(half_pre)
        return (1.0 + half_pre * (1.0 - tanh)) * ((1.0 + tanh) * factor)

    def inner_value(back, pre):
        return slope(pre * params[2] + params[3], back * params[2])

    every = (0, 1, 2)

    def contract(weights, taps, pieces):
        lhs = []
        for i in taps:
            for j in range(3):
                stack = [part for piece in pieces for part in piece(i, j)]
                lhs.append(stack[0] if len(stack) == 1 else jnp.concatenate(stack, 0))
        rhs = weights[taps[0] : taps[-1] + 1].reshape(len(taps) * 3 * chans, chans)
        return jnp.dot(jnp.concatenate(lhs, 1), rhs, preferred_element_type=f32)

    def body(ref, place, count, start, width):
        def piece(i, j):
            part = ref[place + i : place + i + count, (start + j) * TILE : (start + j) * TILE + width]
            return [part.reshape(count * width, chans)]

        return piece

    half = rows // 2
    halves = ((2, half), (2 + half, rows - 2 - half))

    def inner_store(ref, n, value):
        for t in range(step):
            at = pl.ds(n * span + TILE + t, TILE, stride=step)
            put(ref, (at,), value[t * TILE : (t + 1) * TILE])

    def inner_tiles(ref, n, h):
        for t in range(step + 2):
            part = take(ref, (pl.ds(n * span + TILE + t - 1, TILE, stride=step),))
            icat[h, t * TILE : (t + 1) * TILE] = part.astype(bf16)

    def products(place, count):
        back = contract(k2t, every, [body(cat.at[1], place, count, 0, cols)])
        pre = contract(k1, every, [body(cat.at[0], place, count, 0, cols)])
        for n in range(count):
            back_main[place + n] = back[n * cols : (n + 1) * cols]
            pre_main[place + n] = pre[n * cols : (n + 1) * cols]

    def inner_rows(place, count):
        for n in range(place, place + count):
            inner_store(ins, n, inner_value(back_main[n], pre_main[n]))

    load_k2.wait()
    load_k1.wait()
    flip(k2, k2t)
    for h in range(2, rows + 2):
        for m in range(2):
            tiles(m, h, range(step + 2))
    products(*halves[0])

    for m in (1, 0):
        for n in range(2):

            @pl.when(col_there[n])
            def _():
                col_copy(1 - n, m).wait_recv()

    for m in range(2):
        for n in range(2):
            for c in range(NEAR):
                part = col_halo[n, m, c * rows : (c + 1) * rows]
                part = part.astype(f32) if m else activate(part)
                part = jnp.where(col_there[n], part, 0.0)
                put(stage, (m, down(2, (-NEAR, cols)[n] + c)), part)
    def corner_at(d, m, q):
        first = ((2 * d + m) * 2 + q) * NEAR
        return slice(first, first + NEAR)

    for n in range(2):
        for d in range(2):
            for m in range(2):
                for q in range(2):
                    h = (2 + d, rows + 1 - d)[n]
                    corner_f32[n, corner_at(d, m, q)] = take(stage, (m, near(h, q)))
        corner_out[n] = corner_f32[n].astype(bf16)
    for n in range(2):

        @pl.when(row_there[n])
        def _():
            corner_copy(n).start()

    send_row(later, 1, (1, 0))

    products(*halves[1])
    inner_rows(*halves[0])
    flip(k1, k1t)
    send_row(sooner, 1, (1, 0))
    def out_store(at, back):
        for t in range(step):
            put(outs, (pl.ds(at + t, TILE, stride=step),), back[t * TILE : (t + 1) * TILE])

    def finish(n):
        value = take(outs, (slice(n * cols, (n + 1) * cols),)) * gain[n]
        o_ref[0, n] = (value + xg[1, n].astype(f32)).astype(bf16)

    side_cols = (-1, 0, cols - 1, cols)

    def beside(m):
        return lambda i, j: [
            take(stage, (m, down(i + 1, col + j - 1))).astype(bf16) for col in side_cols
        ]

    value = inner_value(contract(k2t, every, [beside(1)]), contract(k1, every, [beside(0)]))
    inner_rows(*halves[1])
    for q, (col, there) in enumerate(zip(side_cols, (left, None, None, right))):
        part = value[q * TILE : q * TILE + rows]
        put(ins, (down(1, col),), part if there is None else jnp.where(there, part, 0.0))
    for n in range(2, rows):
        inner_tiles(ins, n, n)

    half = (rows - 4) // 2
    for place in (2, 2 + half):
        back = contract(k1t, every, [body(icat, place, half, 0, cols)])
        for q in range(half):
            out_store((place + q) * cols, back[q * cols : (q + 1) * cols])

    for n in range(2):

        @pl.when(row_there[n])
        def _():
            row_both(1 - n, 0).wait_recv()
            corner_copy(1 - n).wait_recv()

    def ends_at(h, j):
        return pl.ds(h * span + TILE + j - 2, 2, stride=cols + 1)

    def edge_tiles(n, h):
        for m in range(2):
            for j in range(3):
                place = h - n * rows
                edge_cat[n, m, place, j, :2] = take(stage, (m, ends_at(h, j)))

    def stage_halo(n):
        h = (1, rows + 2)[n]
        for m in range(2):
            value = row_halo[n, 0, m]
            value = value.astype(f32) if m else activate(value)
            put(stage, (m, inside(h)), jnp.where(row_there[n], value, 0.0))
            for q in range(2):
                put(stage, (m, near(h, q)), corner_f32[n, corner_at(0, m, q)])
            tiles(m, h, range(step + 2))
        edge_tiles(n, h)

    def line(n, m, place):
        def piece(i, j):
            ends = edge_cat[n, m, place + i - n * rows, j].astype(bf16)
            return [cat[m, place + i, j * TILE : j * TILE + cols], ends]

        return piece

    place_in = lax.broadcasted_iota(jnp.int32, (TILE, chans), 0)
    ends_ok = jnp.logical_or(
        jnp.logical_and(place_in == 0, left), jnp.logical_and(place_in == 1, right)
    )

    def edge_store(ref, row, place, value):
        main, ends = value[:cols], jnp.where(ends_ok, value[cols:], 0.0)
        inner_store(ref, row, main)
        for q, col in enumerate((-1, cols)):
            at = row * span + TILE + col
            put(ref, (slice(at, at + 1),), ends[q : q + 1])
        inner_tiles(ref, row, place)

    for n in range(2):
        corner_f32[n] = jnp.where(row_there[n], corner_in[n].astype(f32), 0.0)
        stage_halo(n)
        for h in ((2, 3), (rows, rows + 1))[n]:
            for m in range(2):
                tiles(m, h, (0, step + 1))
            edge_tiles(n, h)
    wide = cols + TILE
    places = ((0, 1), (rows + 1, rows))
    lines = [[line(n, m, place) for n in range(2) for place in places[n]] for m in range(2)]
    back = contract(k2t, every, lines[1])
    pre = contract(k1, every, lines[0])
    for n in range(2, rows - 2):
        finish(n)
    for n, (outer, place) in enumerate(places):
        first = 2 * n * wide
        back_part[n] = back[first : first + wide]
        pre_part[n] = pre[first : first + wide]
        first += wide
        edge_store(ins, place, place, inner_value(back[first : first + wide], pre[first : first + wide]))

    for n, place in enumerate((0, rows - 2)):
        back = contract(k1t, every, [body(icat, place, 2, 0, cols)])
        out_edge[n] = back[n * cols : (n + 1) * cols]
        inner = (1, rows - 2)[n]
        out_store(inner * cols, back[(1 - n) * cols : (2 - n) * cols])
        finish(inner)

    def last_rows(n):
        h, outer, place = n * (rows + 3), n * (rows + 1), n * (rows - 1)

        @pl.when(beyond(n))
        def _():
            row_both(1 - n, 1).wait_recv()
            for m in range(2):
                value = row_halo[n, 1, m]
                value = value.astype(f32) if m else activate(value)
                halo = far.at[n, m]
                put(halo, (inside(0),), value)
                for q in range(2):
                    put(halo, (near(0, q),), corner_f32[n, corner_at(1, m, q)])
                for t in range(step + 2):
                    part = take(halo, (pl.ds(TILE + t - 1, TILE, stride=step),))
                    cat[m, h, t * TILE : (t + 1) * TILE] = part.astype(bf16)
                for j in range(3):
                    edge_cat[n, m, 3 * n, j, :2] = take(halo, (ends_at(0, j),))

            def tap(weights, pieces):
                lhs = jnp.concatenate([jnp.concatenate(pieces(j), 0) for j in range(3)], 1)
                rhs = weights[2 * n].reshape(3 * chans, chans)
                return jnp.dot(lhs, rhs, preferred_element_type=f32)

            def ends_line(m):
                return lambda j: [
                    cat[m, h, j * TILE : j * TILE + cols],
                    edge_cat[n, m, 3 * n, j].astype(bf16),
                ]

            back = tap(k2t, ends_line(1)) + back_part[n]
            pre = tap(k1, ends_line(0)) + pre_part[n]
            edge_store(edge_ins.at[n], 0, outer, inner_value(back, pre))
            out_edge[n] += tap(k1t, lambda j: [icat[outer, j * TILE : j * TILE + cols]])

        back = out_edge[n]
        for t in range(step):
            at = pl.ds(t, TILE, stride=step)
            put(edge_outs.at[n], (at,), back[t * TILE : (t + 1) * TILE])
        value = take(edge_outs.at[n], (slice(0, cols),)) * gain[place]
        o_ref[0, place] = (value + xg[1, place].astype(f32)).astype(bf16)

    last_rows(sooner)
    @pl.when(beyond(later))
    def _():
        row_both(1 - later, 1).wait_recv()
        last_halo[...] = row_halo[later, 1]

    for n in range(2):

        @pl.when(row_there[n])
        def _():
            for d in range(2):
                row_both(n, d).wait_send()
            corner_copy(n).wait_send()

        @pl.when(col_there[n])
        def _():
            for m in range(2):
                col_copy(n, m).wait_send()


def hand_over(
    rows,
    cols,
    chans,
    o_in,
    k1,
    k2t,
    k1t,
    params,
    gain,
    xg,
    back_part,
    pre_part,
    out_edge,
    corner_f32,
    last_halo,
    target,
    stage,
    ins,
    cat,
    edge_cat,
    icat,
    outs,
    total,
    last,
    sem,
):
    span, step = cols + 2 * TILE, cols // TILE
    lane_parts = [slice(k, k + LANES) for k in range(0, chans, LANES)]
    f32, bf16 = jnp.float32, jnp.bfloat16
    my_row, n_rows = lax.axis_index("rows"), lax.axis_size("rows")
    my_col, n_cols = lax.axis_index("cols"), lax.axis_size("cols")
    n = 1 - my_row % 2
    place = n * (rows - 1)
    most = pl.ds(1 - n, rows - 1)
    early = pltpu.make_async_copy(o_in.at[0, most], target.at[0, most], sem.at[0])
    early.start()

    def put(ref, at, value):
        for k, lanes in enumerate(lane_parts):
            ref[k, at] = value[:, lanes]

    def take(ref, at):
        return jnp.concatenate([ref[k, at] for k in range(len(lane_parts))], 1)

    def tap(weights, pieces):
        lhs = jnp.concatenate([jnp.concatenate(pieces(j), 0) for j in range(3)], 1)
        rhs = weights[2 * n].reshape(3 * chans, chans)
        return jnp.dot(lhs, rhs, preferred_element_type=f32)

    total[...] = out_edge[n]
    there = jnp.logical_and(my_row + 2 * n >= 1, my_row + 2 * n < n_rows + 1)

    @pl.when(there)
    def _():
        for m in range(2):
            value = last_halo[m].astype(f32)
            if m == 0:
                value = value * params[0] + params[1]
                value = value * (1.0 + jnp.tanh(value))
            halo = stage.at[m]
            put(halo, slice(TILE, TILE + cols), value)
            for q, at in enumerate((TILE - NEAR, TILE + cols)):
                first = ((2 + m) * 2 + q) * NEAR
                put(halo, slice(at, at + NEAR), corner_f32[n, first : first + NEAR])
            for t in range(step + 2):
                part = take(halo, pl.ds(TILE + t - 1, TILE, stride=step))
                cat[m, t * TILE : (t + 1) * TILE] = part.astype(bf16)
            for j in range(3):
                ends = pl.ds(TILE + j - 2, 2, stride=cols + 1)
                edge_cat[m, j] = jnp.zeros((TILE, chans), f32)
                edge_cat[m, j, :2] = take(halo, ends)

        def line(m):
            return lambda j: [
                cat[m, j * TILE : j * TILE + cols],
                edge_cat[m, j].astype(bf16),
            ]

        back = (tap(k2t, line(1)) + back_part[n]) * params[2]
        pre = (tap(k1, line(0)) + pre_part[n]) * params[2] + params[3]
        tanh = jnp.tanh(pre)
        value = (1.0 + pre * (1.0 - tanh)) * ((1.0 + tanh) * back)
        for t in range(step):
            at = pl.ds(TILE + t, TILE, stride=step)
            put(ins, at, value[t * TILE : (t + 1) * TILE])
        for q, (at, ok) in enumerate(((TILE - 1, my_col > 0), (TILE + cols, my_col < n_cols - 1))):
            put(ins, slice(at, at + 1), jnp.where(ok, value[cols + q : cols + q + 1], 0.0))
        for t in range(step + 2):
            part = take(ins, pl.ds(TILE + t - 1, TILE, stride=step))
            icat[t * TILE : (t + 1) * TILE] = part.astype(bf16)
        lhs = jnp.concatenate([icat[j * TILE : j * TILE + cols] for j in range(3)], 1)
        rhs = k1t[2 * n].reshape(3 * chans, chans)
        half = cols // 2
        for at in (0, half):
            part = jnp.dot(lhs[at : at + half], rhs, preferred_element_type=f32)
            total[at : at + half] += part

    for t in range(step):
        put(outs, pl.ds(t, TILE, stride=step), total[t * TILE : (t + 1) * TILE])
    value = take(outs, slice(0, cols)) * gain[place] + xg[1, place].astype(f32)
    last[...] = value.astype(bf16)
    late = pltpu.make_async_copy(last, target.at[0, place], sem.at[1])
    late.start()
    early.wait()
    late.wait()


def per_device(
    image_in,
    cotangent,
    first_kernel,
    first_bias,
    second_kernel,
    first_center,
    first_inverse,
    first_gain,
    first_shift,
    second_center,
    second_inverse,
    second_gain,
    second_shift,
):
    _, rows, cols, chans = image_in.shape
    groups = first_center.shape[0]
    span, step = cols + 2 * TILE, cols // TILE
    lanes = chans // LANES
    bf16, f32 = jnp.bfloat16, jnp.float32
    vec = lambda v: v.reshape(1, chans)
    result = pl.pallas_call(
        functools.partial(kernel, rows, cols, chans, groups),
        out_shape=(
            jax.ShapeDtypeStruct(image_in.shape, bf16),
            jax.ShapeDtypeStruct((3, 3, chans, chans), bf16),
            jax.ShapeDtypeStruct((3, 3, chans, chans), bf16),
            jax.ShapeDtypeStruct((3, 3, chans, chans), bf16),
            jax.ShapeDtypeStruct((4, 1, chans), f32),
            jax.ShapeDtypeStruct((rows, cols, chans), f32),
            jax.ShapeDtypeStruct((2, rows, cols, chans), bf16),
            jax.ShapeDtypeStruct((2, cols + TILE, chans), f32),
            jax.ShapeDtypeStruct((2, cols + TILE, chans), f32),
            jax.ShapeDtypeStruct((2, cols, chans), f32),
            jax.ShapeDtypeStruct((2, TILE, chans), f32),
            jax.ShapeDtypeStruct((2, cols, chans), bf16),
        ),
        in_specs=[pl.BlockSpec(memory_space=pltpu.HBM)] * 13,
        out_specs=(pl.BlockSpec(memory_space=pltpu.VMEM),) * 12,
        scratch_shapes=[
            pltpu.VMEM((3, 3, chans, chans), bf16),
            pltpu.VMEM((5, 1, chans), f32),
            pltpu.SMEM((4, groups), f32),
            pltpu.VMEM((2, lanes, (rows + 4) * span, LANES), f32),
            pltpu.VMEM((2, 2, lanes, rows * TILE, LANES), f32),
            pltpu.VMEM((2, 2, lanes, span, LANES), f32),
            pltpu.VMEM((lanes, (rows + 2) * span, LANES), f32),
            pltpu.VMEM((2, lanes, span, LANES), f32),
            pltpu.VMEM((lanes, rows * cols, LANES), f32),
            pltpu.VMEM((2, lanes, cols, LANES), f32),
            pltpu.VMEM((2, rows + 4, (step + 2) * TILE, chans), bf16),
            pltpu.VMEM((2, 2, 4, 3, TILE, chans), f32),
            pltpu.VMEM((rows + 2, (step + 2) * TILE, chans), bf16),
            pltpu.VMEM((rows + 2, cols, chans), f32),
            pltpu.VMEM((rows + 2, cols, chans), f32),
            pltpu.VMEM((2, 2, 2, cols, chans), bf16),
            pltpu.VMEM((2, 2, NEAR * rows, chans), bf16),
            pltpu.VMEM((2, 2, NEAR * rows, chans), bf16),
            pltpu.VMEM((2, TILE, chans), bf16),
            pltpu.VMEM((2, TILE, chans), bf16),
            pltpu.SemaphoreType.DMA((9,)),
            pltpu.SemaphoreType.DMA((2, 2)),
            pltpu.SemaphoreType.DMA((2, 2)),
            pltpu.SemaphoreType.DMA((2, 2)),
            pltpu.SemaphoreType.DMA((2, 2)),
            pltpu.SemaphoreType.DMA((2,)),
            pltpu.SemaphoreType.DMA((2,)),
        ],
        compiler_params=pltpu.CompilerParams(
            collective_id=0, has_side_effects=True, vmem_limit_bytes=40 << 20
        ),
    )(
        *(
            pltpu.with_memory_space_constraint(value, pltpu.HBM)
            for value in (
                image_in,
                cotangent,
                first_kernel,
                vec(first_bias),
                second_kernel,
                first_center,
                first_inverse,
                vec(first_gain),
                vec(first_shift),
                second_center,
                second_inverse,
                vec(second_gain),
                vec(second_shift),
            )
        )
    )
    return pl.pallas_call(
        functools.partial(hand_over, rows, cols, chans),
        out_shape=jax.ShapeDtypeStruct(image_in.shape, bf16),
        in_specs=[pl.BlockSpec(memory_space=pltpu.VMEM)] * len(result),
        out_specs=pl.BlockSpec(memory_space=pltpu.HBM),
        scratch_shapes=[
            pltpu.VMEM((2, lanes, span, LANES), f32),
            pltpu.VMEM((lanes, span, LANES), f32),
            pltpu.VMEM((2, (step + 2) * TILE, chans), bf16),
            pltpu.VMEM((2, 3, TILE, chans), f32),
            pltpu.VMEM(((step + 2) * TILE, chans), bf16),
            pltpu.VMEM((lanes, cols, LANES), f32),
            pltpu.VMEM((cols, chans), f32),
            pltpu.VMEM((cols, chans), bf16),
            pltpu.SemaphoreType.DMA((2,)),
        ],
        compiler_params=pltpu.CompilerParams(vmem_limit_bytes=8 << 20),
    )(*result)


def solution(mesh):
    return jax.shard_map(
        per_device,
        mesh=mesh,
        in_specs=(P(None, "rows", "cols", None),) * 2 + (P(),) * 11,
        out_specs=P(None, "rows", "cols", None),
        check_vma=False,
    )
```

```python
import functools

import jax
import jax.numpy as jnp
from jax import lax
from jax.experimental import pallas as pl
from jax.experimental.pallas import tpu as pltpu
from jax.sharding import PartitionSpec as P

MESH = pl.DeviceIdType.MESH
TILE = 16
LANES = 128
NEAR = 2
SIDES = (-1, 1)


def kernel(
    rows,
    cols,
    chans,
    groups,
    x_hbm,
    g_hbm,
    k1_hbm,
    b1_hbm,
    k2_hbm,
    c1_hbm,
    v1_hbm,
    n1_hbm,
    s1_hbm,
    c2_hbm,
    v2_hbm,
    n2_hbm,
    s2_hbm,
    o_ref,
    k1,
    k2t,
    k1t,
    params,
    gain,
    xg,
    back_part,
    pre_part,
    out_edge,
    corner_f32,
    last_halo,
    k2,
    vecs,
    scal,
    stage,
    raw,
    far,
    ins,
    edge_ins,
    outs,
    edge_outs,
    cat,
    edge_cat,
    icat,
    back_main,
    pre_main,
    row_halo,
    pack,
    col_halo,
    corner_out,
    corner_in,
    load_sem,
    row_send,
    row_recv,
    col_send,
    col_recv,
    corner_send,
    corner_recv,
):
    span = cols + 2 * TILE
    step = cols // TILE
    lane_parts = [slice(k, k + LANES) for k in range(0, chans, LANES)]
    f32, bf16 = jnp.float32, jnp.bfloat16
    my_row, my_col = lax.axis_index("rows"), lax.axis_index("cols")
    n_rows, n_cols = lax.axis_size("rows"), lax.axis_size("cols")
    above, below = my_row > 0, my_row < n_rows - 1
    left, right = my_col > 0, my_col < n_cols - 1
    row_there, col_there = (above, below), (left, right)

    barrier = pltpu.get_barrier_semaphore()
    for n, side in enumerate(SIDES):

        @pl.when(col_there[n])
        def _():
            pl.semaphore_signal(
                barrier, inc=1, device_id=(my_row, my_col + side), device_id_type=MESH
            )

        @pl.when(row_there[n])
        def _():
            pl.semaphore_signal(
                barrier, inc=1, device_id=(my_row + side, my_col), device_id_type=MESH
            )

    load_k2 = pltpu.make_async_copy(k2_hbm, k2, load_sem.at[0])
    load_k1 = pltpu.make_async_copy(k1_hbm, k1, load_sem.at[1])
    load_x = pltpu.make_async_copy(x_hbm.at[0], xg.at[0], load_sem.at[2])
    load_g = pltpu.make_async_copy(g_hbm.at[0], xg.at[1], load_sem.at[3])
    load_g.start()
    load_x.start()
    for n, ref in enumerate((b1_hbm, n1_hbm, s1_hbm, n2_hbm, s2_hbm)):
        pltpu.make_async_copy(ref, vecs.at[n], load_sem.at[4]).start()
    for n, ref in enumerate((c1_hbm, v1_hbm, c2_hbm, v2_hbm)):
        pltpu.make_async_copy(ref, scal.at[n], load_sem.at[5 + n]).start()
    load_k2.start()
    load_k1.start()

    def one(there):
        return jnp.where(there, 1, 0)


    def row_link(n, d, src, dst):
        return pltpu.make_async_remote_copy(
            src_ref=src,
            dst_ref=dst,
            send_sem=row_send.at[n, d],
            recv_sem=row_recv.at[1 - n, d],
            device_id=(my_row + 2 * n - 1, my_col),
            device_id_type=MESH,
        )

    def beyond(n):
        return jnp.logical_and(my_row + 2 * n >= 1, my_row + 2 * n < n_rows + 1)

    def send_row(n, d, which):
        @pl.when(beyond(n))
        def _():
            for m in which:
                src = (x_hbm, g_hbm)[m].at[0, d + n * (rows - 1 - 2 * d)]
                row_link(n, d, src, row_halo.at[1 - n, d, m]).start()

    sooner = my_row % 2
    later = 1 - sooner

    def row_both(n, d):
        return row_link(n, d, row_halo.at[1 - n, d], row_halo.at[1 - n, d])

    def col_copy(n, m):
        return pltpu.make_async_remote_copy(
            src_ref=pack.at[n, m],
            dst_ref=col_halo.at[1 - n, m],
            send_sem=col_send.at[n, m],
            recv_sem=col_recv.at[1 - n, m],
            device_id=(my_row, my_col + SIDES[n]),
            device_id_type=MESH,
        )

    def corner_copy(n):
        return pltpu.make_async_remote_copy(
            src_ref=corner_out.at[n],
            dst_ref=corner_in.at[1 - n],
            send_sem=corner_send.at[n],
            recv_sem=corner_recv.at[1 - n],
            device_id=(my_row + SIDES[n], my_col),
            device_id_type=MESH,
        )


    def flip(source, target):
        for i in range(3):
            for j in range(3):
                target[i, j] = source[2 - i, 2 - j].T

    def put(ref, at, value):
        for k, lanes in enumerate(lane_parts):
            ref[(*at[:-1], k, at[-1])] = value[:, lanes]

    def take(ref, at):
        return jnp.concatenate([ref[(*at[:-1], k, at[-1])] for k in range(len(lane_parts))], 1)

    def near(h, n):
        first = h * span + (TILE - NEAR, TILE + cols)[n]
        return slice(first, first + NEAR)

    def inside(h):
        return slice(h * span + TILE, h * span + TILE + cols)

    def down(h, col):
        return pl.ds(h * span + TILE + col, rows, stride=span)

    def tiles(m, h, which):
        for t in which:
            part = take(stage, (m, pl.ds(h * span + TILE + t - 1, TILE, stride=step)))
            cat[m, h, t * TILE : (t + 1) * TILE] = part.astype(bf16)

    def pack_cols(m):
        for n in range(2):
            for r in range(rows):
                tile = xg[m, r, (0, cols - TILE)[n] : (TILE, cols)[n]].astype(f32)
                put(raw, (n, m, slice(r * TILE, (r + 1) * TILE)), tile)
            for c in range(NEAR):
                column = pl.ds((0, TILE - NEAR)[n] + c, rows, stride=TILE)
                part = take(raw, (n, m, column))
                pack[n, m, c * rows : (c + 1) * rows] = part.astype(bf16)

    def send_cols(m):
        for n in range(2):

            @pl.when(col_there[n])
            def _():
                col_copy(n, m).start()

    for h in (0, rows + 1):
        icat[h] = jnp.zeros(icat.shape[1:], bf16)
    for h in (0, rows + 3):
        for m in range(2):
            cat[m, h] = jnp.zeros(cat.shape[2:], bf16)
    edge_cat[...] = jnp.zeros(edge_cat.shape, f32)

    load_g.wait()
    for n in range(rows):
        put(stage, (1, inside(n + 2)), xg[1, n].astype(f32))
    pack_cols(1)
    pltpu.make_async_copy(vecs, vecs, load_sem.at[4]).wait()
    for n, ref in enumerate((c1_hbm, v1_hbm, c2_hbm, v2_hbm)):
        pltpu.make_async_copy(ref, scal.at[n], load_sem.at[5 + n]).wait()
    lane_group = lax.broadcasted_iota(jnp.int32, (1, chans), 1) // (chans // groups)

    def spread(n):
        total = jnp.zeros((1, chans), f32)
        for q in range(groups):
            total = jnp.where(lane_group == q, scal[n, q], total)
        return total

    scale1 = spread(1) * vecs[1]
    scale2 = spread(3) * vecs[3]
    params[0] = 0.5 * scale1
    params[1] = 0.5 * (vecs[2] - spread(0) * scale1)
    params[2] = 0.5 * scale2
    params[3] = 0.5 * ((vecs[0] - spread(2)) * scale2 + vecs[4])

    pl.semaphore_wait(barrier, one(above) + one(below) + one(left) + one(right))
    for n in range(2):
        send_row(n, 0, (1,))
    send_cols(1)
    load_x.wait()
    pack_cols(0)
    send_cols(0)
    for n in range(2):
        send_row(n, 0, (0,))

    def activate(value):
        half_pre = value.astype(f32) * params[0] + params[1]
        return half_pre * (1.0 + jnp.tanh(half_pre))

    for n in range(rows):
        half_pre = xg[0, n].astype(f32) * params[0] + params[1]
        more = 1.0 + jnp.tanh(half_pre)
        act = half_pre * more
        put(stage, (0, inside(n + 2)), act)
        gain[n] = (1.0 + half_pre + half_pre - act) * (more * params[0])

    def slope(half_pre, factor):
        tanh = jnp.tanh(half_pre)
        return (1.0 + half_pre * (1.0 - tanh)) * ((1.0 + tanh) * factor)

    def inner_value(back, pre):
        return slope(pre * params[2] + params[3], back * params[2])

    every = (0, 1, 2)

    def contract(weights, taps, pieces):
        lhs = []
        for i in taps:
            for j in range(3):
                stack = [part for piece in pieces for part in piece(i, j)]
                lhs.append(stack[0] if len(stack) == 1 else jnp.concatenate(stack, 0))
        rhs = weights[taps[0] : taps[-1] + 1].reshape(len(taps) * 3 * chans, chans)
        return jnp.dot(jnp.concatenate(lhs, 1), rhs, preferred_element_type=f32)

    def body(ref, place, count, start, width):
        def piece(i, j):
            part = ref[place + i : place + i + count, (start + j) * TILE : (start + j) * TILE + width]
            return [part.reshape(count * width, chans)]

        return piece

    half = rows // 2 + 1
    halves = ((2, half), (2 + half, rows - 2 - half))

    def inner_store(ref, n, value):
        for t in range(step):
            at = pl.ds(n * span + TILE + t, TILE, stride=step)
            put(ref, (at,), value[t * TILE : (t + 1) * TILE])

    def inner_tiles(ref, n, h):
        for t in range(step + 2):
            part = take(ref, (pl.ds(n * span + TILE + t - 1, TILE, stride=step),))
            icat[h, t * TILE : (t + 1) * TILE] = part.astype(bf16)

    def products(place, count):
        back = contract(k2t, every, [body(cat.at[1], place, count, 0, cols)])
        pre = contract(k1, every, [body(cat.at[0], place, count, 0, cols)])
        for n in range(count):
            back_main[place + n] = back[n * cols : (n + 1) * cols]
            pre_main[place + n] = pre[n * cols : (n + 1) * cols]

    def inner_rows(place, count):
        for n in range(place, place + count):
            inner_store(ins, n, inner_value(back_main[n], pre_main[n]))

    load_k2.wait()
    load_k1.wait()
    flip(k2, k2t)
    for h in range(2, rows + 2):
        for m in range(2):
            tiles(m, h, range(step + 2))
    products(*halves[0])

    for m in (1, 0):
        for n in range(2):

            @pl.when(col_there[n])
            def _():
                col_copy(1 - n, m).wait_recv()

    for m in range(2):
        for n in range(2):
            for c in range(NEAR):
                part = col_halo[n, m, c * rows : (c + 1) * rows]
                part = part.astype(f32) if m else activate(part)
                part = jnp.where(col_there[n], part, 0.0)
                put(stage, (m, down(2, (-NEAR, cols)[n] + c)), part)
    def corner_at(d, m, q):
        first = ((2 * d + m) * 2 + q) * NEAR
        return slice(first, first + NEAR)

    for n in range(2):
        for d in range(2):
            for m in range(2):
                for q in range(2):
                    h = (2 + d, rows + 1 - d)[n]
                    corner_f32[n, corner_at(d, m, q)] = take(stage, (m, near(h, q)))
        corner_out[n] = corner_f32[n].astype(bf16)
    for n in range(2):

        @pl.when(row_there[n])
        def _():
            corner_copy(n).start()

    send_row(later, 1, (1, 0))

    products(*halves[1])
    inner_rows(*halves[0])
    flip(k1, k1t)
    send_row(sooner, 1, (1, 0))
    def out_store(at, back):
        for t in range(step):
            put(outs, (pl.ds(at + t, TILE, stride=step),), back[t * TILE : (t + 1) * TILE])

    def finish(n):
        value = take(outs, (slice(n * cols, (n + 1) * cols),)) * gain[n]
        o_ref[0, n] = (value + xg[1, n].astype(f32)).astype(bf16)

    side_cols = (-1, 0, cols - 1, cols)

    def beside(m):
        return lambda i, j: [
            take(stage, (m, down(i + 1, col + j - 1))).astype(bf16) for col in side_cols
        ]

    value = inner_value(contract(k2t, every, [beside(1)]), contract(k1, every, [beside(0)]))
    inner_rows(*halves[1])
    for q, (col, there) in enumerate(zip(side_cols, (left, None, None, right))):
        part = value[q * TILE : q * TILE + rows]
        put(ins, (down(1, col),), part if there is None else jnp.where(there, part, 0.0))
    for n in range(2, rows):
        inner_tiles(ins, n, n)

    half = (rows - 4) // 2
    for place in (2, 2 + half):
        back = contract(k1t, every, [body(icat, place, half, 0, cols)])
        for q in range(half):
            out_store((place + q) * cols, back[q * cols : (q + 1) * cols])

    for n in range(2):

        @pl.when(row_there[n])
        def _():
            row_both(1 - n, 0).wait_recv()
            corner_copy(1 - n).wait_recv()

    def ends_at(h, j):
        return pl.ds(h * span + TILE + j - 2, 2, stride=cols + 1)

    def edge_tiles(n, h):
        for m in range(2):
            for j in range(3):
                place = h - n * rows
                edge_cat[n, m, place, j, :2] = take(stage, (m, ends_at(h, j)))

    def stage_halo(n):
        h = (1, rows + 2)[n]
        for m in range(2):
            value = row_halo[n, 0, m]
            value = value.astype(f32) if m else activate(value)
            put(stage, (m, inside(h)), jnp.where(row_there[n], value, 0.0))
            for q in range(2):
                put(stage, (m, near(h, q)), corner_f32[n, corner_at(0, m, q)])
            tiles(m, h, range(step + 2))
        edge_tiles(n, h)

    def line(n, m, place):
        def piece(i, j):
            ends = edge_cat[n, m, place + i - n * rows, j].astype(bf16)
            return [cat[m, place + i, j * TILE : j * TILE + cols], ends]

        return piece

    place_in = lax.broadcasted_iota(jnp.int32, (TILE, chans), 0)
    ends_ok = jnp.logical_or(
        jnp.logical_and(place_in == 0, left), jnp.logical_and(place_in == 1, right)
    )

    def edge_store(ref, row, place, value):
        main, ends = value[:cols], jnp.where(ends_ok, value[cols:], 0.0)
        inner_store(ref, row, main)
        for q, col in enumerate((-1, cols)):
            at = row * span + TILE + col
            put(ref, (slice(at, at + 1),), ends[q : q + 1])
        inner_tiles(ref, row, place)

    for n in range(2):
        corner_f32[n] = jnp.where(row_there[n], corner_in[n].astype(f32), 0.0)
        stage_halo(n)
        for h in ((2, 3), (rows, rows + 1))[n]:
            for m in range(2):
                tiles(m, h, (0, step + 1))
            edge_tiles(n, h)
    wide = cols + TILE
    places = ((0, 1), (rows + 1, rows))
    lines = [[line(n, m, place) for n in range(2) for place in places[n]] for m in range(2)]
    back = contract(k2t, every, lines[1])
    pre = contract(k1, every, lines[0])
    for n in range(2, rows - 2):
        finish(n)
    for n, (outer, place) in enumerate(places):
        first = 2 * n * wide
        back_part[n] = back[first : first + wide]
        pre_part[n] = pre[first : first + wide]
        first += wide
        edge_store(ins, place, place, inner_value(back[first : first + wide], pre[first : first + wide]))

    for n, place in enumerate((0, rows - 2)):
        back = contract(k1t, every, [body(icat, place, 2, 0, cols)])
        out_edge[n] = back[n * cols : (n + 1) * cols]
        inner = (1, rows - 2)[n]
        out_store(inner * cols, back[(1 - n) * cols : (2 - n) * cols])
        finish(inner)

    def last_rows(n):
        h, outer, place = n * (rows + 3), n * (rows + 1), n * (rows - 1)

        @pl.when(beyond(n))
        def _():
            row_both(1 - n, 1).wait_recv()
            for m in range(2):
                value = row_halo[n, 1, m]
                value = value.astype(f32) if m else activate(value)
                halo = far.at[n, m]
                put(halo, (inside(0),), value)
                for q in range(2):
                    put(halo, (near(0, q),), corner_f32[n, corner_at(1, m, q)])
                for t in range(step + 2):
                    part = take(halo, (pl.ds(TILE + t - 1, TILE, stride=step),))
                    cat[m, h, t * TILE : (t + 1) * TILE] = part.astype(bf16)
                for j in range(3):
                    edge_cat[n, m, 3 * n, j, :2] = take(halo, (ends_at(0, j),))

            def tap(weights, pieces):
                lhs = jnp.concatenate([jnp.concatenate(pieces(j), 0) for j in range(3)], 1)
                rhs = weights[2 * n].reshape(3 * chans, chans)
                return jnp.dot(lhs, rhs, preferred_element_type=f32)

            def ends_line(m):
                return lambda j: [
                    cat[m, h, j * TILE : j * TILE + cols],
                    edge_cat[n, m, 3 * n, j].astype(bf16),
                ]

            back = tap(k2t, ends_line(1)) + back_part[n]
            pre = tap(k1, ends_line(0)) + pre_part[n]
            edge_store(edge_ins.at[n], 0, outer, inner_value(back, pre))
            out_edge[n] += tap(k1t, lambda j: [icat[outer, j * TILE : j * TILE + cols]])

        back = out_edge[n]
        for t in range(step):
            at = pl.ds(t, TILE, stride=step)
            put(edge_outs.at[n], (at,), back[t * TILE : (t + 1) * TILE])
        value = take(edge_outs.at[n], (slice(0, cols),)) * gain[place]
        o_ref[0, place] = (value + xg[1, place].astype(f32)).astype(bf16)

    last_rows(sooner)
    @pl.when(beyond(later))
    def _():
        row_both(1 - later, 1).wait_recv()
        last_halo[...] = row_halo[later, 1]

    for n in range(2):

        @pl.when(row_there[n])
        def _():
            for d in range(2):
                row_both(n, d).wait_send()
            corner_copy(n).wait_send()

        @pl.when(col_there[n])
        def _():
            for m in range(2):
                col_copy(n, m).wait_send()


def hand_over(
    rows,
    cols,
    chans,
    o_in,
    k1,
    k2t,
    k1t,
    params,
    gain,
    xg,
    back_part,
    pre_part,
    out_edge,
    corner_f32,
    last_halo,
    target,
    stage,
    ins,
    cat,
    edge_cat,
    icat,
    outs,
    total,
    last,
    sem,
):
    span, step = cols + 2 * TILE, cols // TILE
    lane_parts = [slice(k, k + LANES) for k in range(0, chans, LANES)]
    f32, bf16 = jnp.float32, jnp.bfloat16
    my_row, n_rows = lax.axis_index("rows"), lax.axis_size("rows")
    my_col, n_cols = lax.axis_index("cols"), lax.axis_size("cols")
    n = 1 - my_row % 2
    place = n * (rows - 1)
    most = pl.ds(1 - n, rows - 1)
    early = pltpu.make_async_copy(o_in.at[0, most], target.at[0, most], sem.at[0])
    early.start()

    def put(ref, at, value):
        for k, lanes in enumerate(lane_parts):
            ref[k, at] = value[:, lanes]

    def take(ref, at):
        return jnp.concatenate([ref[k, at] for k in range(len(lane_parts))], 1)

    def tap(weights, pieces):
        lhs = jnp.concatenate([jnp.concatenate(pieces(j), 0) for j in range(3)], 1)
        rhs = weights[2 * n].reshape(3 * chans, chans)
        return jnp.dot(lhs, rhs, preferred_element_type=f32)

    total[...] = out_edge[n]
    there = jnp.logical_and(my_row + 2 * n >= 1, my_row + 2 * n < n_rows + 1)

    @pl.when(there)
    def _():
        for m in range(2):
            value = last_halo[m].astype(f32)
            if m == 0:
                value = value * params[0] + params[1]
                value = value * (1.0 + jnp.tanh(value))
            halo = stage.at[m]
            put(halo, slice(TILE, TILE + cols), value)
            for q, at in enumerate((TILE - NEAR, TILE + cols)):
                first = ((2 + m) * 2 + q) * NEAR
                put(halo, slice(at, at + NEAR), corner_f32[n, first : first + NEAR])
            for t in range(step + 2):
                part = take(halo, pl.ds(TILE + t - 1, TILE, stride=step))
                cat[m, t * TILE : (t + 1) * TILE] = part.astype(bf16)
            for j in range(3):
                ends = pl.ds(TILE + j - 2, 2, stride=cols + 1)
                edge_cat[m, j] = jnp.zeros((TILE, chans), f32)
                edge_cat[m, j, :2] = take(halo, ends)

        def line(m):
            return lambda j: [
                cat[m, j * TILE : j * TILE + cols],
                edge_cat[m, j].astype(bf16),
            ]

        back = (tap(k2t, line(1)) + back_part[n]) * params[2]
        pre = (tap(k1, line(0)) + pre_part[n]) * params[2] + params[3]
        tanh = jnp.tanh(pre)
        value = (1.0 + pre * (1.0 - tanh)) * ((1.0 + tanh) * back)
        for t in range(step):
            at = pl.ds(TILE + t, TILE, stride=step)
            put(ins, at, value[t * TILE : (t + 1) * TILE])
        for q, (at, ok) in enumerate(((TILE - 1, my_col > 0), (TILE + cols, my_col < n_cols - 1))):
            put(ins, slice(at, at + 1), jnp.where(ok, value[cols + q : cols + q + 1], 0.0))
        for t in range(step + 2):
            part = take(ins, pl.ds(TILE + t - 1, TILE, stride=step))
            icat[t * TILE : (t + 1) * TILE] = part.astype(bf16)
        lhs = jnp.concatenate([icat[j * TILE : j * TILE + cols] for j in range(3)], 1)
        rhs = k1t[2 * n].reshape(3 * chans, chans)
        half = cols // 2
        for at in (0, half):
            part = jnp.dot(lhs[at : at + half], rhs, preferred_element_type=f32)
            total[at : at + half] += part

    for t in range(step):
        put(outs, pl.ds(t, TILE, stride=step), total[t * TILE : (t + 1) * TILE])
    value = take(outs, slice(0, cols)) * gain[place] + xg[1, place].astype(f32)
    last[...] = value.astype(bf16)
    late = pltpu.make_async_copy(last, target.at[0, place], sem.at[1])
    late.start()
    early.wait()
    late.wait()


def per_device(
    image_in,
    cotangent,
    first_kernel,
    first_bias,
    second_kernel,
    first_center,
    first_inverse,
    first_gain,
    first_shift,
    second_center,
    second_inverse,
    second_gain,
    second_shift,
):
    _, rows, cols, chans = image_in.shape
    groups = first_center.shape[0]
    span, step = cols + 2 * TILE, cols // TILE
    lanes = chans // LANES
    bf16, f32 = jnp.bfloat16, jnp.float32
    vec = lambda v: v.reshape(1, chans)
    result = pl.pallas_call(
        functools.partial(kernel, rows, cols, chans, groups),
        out_shape=(
            jax.ShapeDtypeStruct(image_in.shape, bf16),
            jax.ShapeDtypeStruct((3, 3, chans, chans), bf16),
            jax.ShapeDtypeStruct((3, 3, chans, chans), bf16),
            jax.ShapeDtypeStruct((3, 3, chans, chans), bf16),
            jax.ShapeDtypeStruct((4, 1, chans), f32),
            jax.ShapeDtypeStruct((rows, cols, chans), f32),
            jax.ShapeDtypeStruct((2, rows, cols, chans), bf16),
            jax.ShapeDtypeStruct((2, cols + TILE, chans), f32),
            jax.ShapeDtypeStruct((2, cols + TILE, chans), f32),
            jax.ShapeDtypeStruct((2, cols, chans), f32),
            jax.ShapeDtypeStruct((2, TILE, chans), f32),
            jax.ShapeDtypeStruct((2, cols, chans), bf16),
        ),
        in_specs=[pl.BlockSpec(memory_space=pltpu.HBM)] * 13,
        out_specs=(pl.BlockSpec(memory_space=pltpu.VMEM),) * 12,
        scratch_shapes=[
            pltpu.VMEM((3, 3, chans, chans), bf16),
            pltpu.VMEM((5, 1, chans), f32),
            pltpu.SMEM((4, groups), f32),
            pltpu.VMEM((2, lanes, (rows + 4) * span, LANES), f32),
            pltpu.VMEM((2, 2, lanes, rows * TILE, LANES), f32),
            pltpu.VMEM((2, 2, lanes, span, LANES), f32),
            pltpu.VMEM((lanes, (rows + 2) * span, LANES), f32),
            pltpu.VMEM((2, lanes, span, LANES), f32),
            pltpu.VMEM((lanes, rows * cols, LANES), f32),
            pltpu.VMEM((2, lanes, cols, LANES), f32),
            pltpu.VMEM((2, rows + 4, (step + 2) * TILE, chans), bf16),
            pltpu.VMEM((2, 2, 4, 3, TILE, chans), f32),
            pltpu.VMEM((rows + 2, (step + 2) * TILE, chans), bf16),
            pltpu.VMEM((rows + 2, cols, chans), f32),
            pltpu.VMEM((rows + 2, cols, chans), f32),
            pltpu.VMEM((2, 2, 2, cols, chans), bf16),
            pltpu.VMEM((2, 2, NEAR * rows, chans), bf16),
            pltpu.VMEM((2, 2, NEAR * rows, chans), bf16),
            pltpu.VMEM((2, TILE, chans), bf16),
            pltpu.VMEM((2, TILE, chans), bf16),
            pltpu.SemaphoreType.DMA((9,)),
            pltpu.SemaphoreType.DMA((2, 2)),
            pltpu.SemaphoreType.DMA((2, 2)),
            pltpu.SemaphoreType.DMA((2, 2)),
            pltpu.SemaphoreType.DMA((2, 2)),
            pltpu.SemaphoreType.DMA((2,)),
            pltpu.SemaphoreType.DMA((2,)),
        ],
        compiler_params=pltpu.CompilerParams(
            collective_id=0, has_side_effects=True, vmem_limit_bytes=40 << 20
        ),
    )(
        *(
            pltpu.with_memory_space_constraint(value, pltpu.HBM)
            for value in (
                image_in,
                cotangent,
                first_kernel,
                vec(first_bias),
                second_kernel,
                first_center,
                first_inverse,
                vec(first_gain),
                vec(first_shift),
                second_center,
                second_inverse,
                vec(second_gain),
                vec(second_shift),
            )
        )
    )
    return pl.pallas_call(
        functools.partial(hand_over, rows, cols, chans),
        out_shape=jax.ShapeDtypeStruct(image_in.shape, bf16),
        in_specs=[pl.BlockSpec(memory_space=pltpu.VMEM)] * len(result),
        out_specs=pl.BlockSpec(memory_space=pltpu.HBM),
        scratch_shapes=[
            pltpu.VMEM((2, lanes, span, LANES), f32),
            pltpu.VMEM((lanes, span, LANES), f32),
            pltpu.VMEM((2, (step + 2) * TILE, chans), bf16),
            pltpu.VMEM((2, 3, TILE, chans), f32),
            pltpu.VMEM(((step + 2) * TILE, chans), bf16),
            pltpu.VMEM((lanes, cols, LANES), f32),
            pltpu.VMEM((cols, chans), f32),
            pltpu.VMEM((cols, chans), bf16),
            pltpu.SemaphoreType.DMA((2,)),
        ],
        compiler_params=pltpu.CompilerParams(vmem_limit_bytes=8 << 20),
    )(*result)


def solution(mesh):
    return jax.shard_map(
        per_device,
        mesh=mesh,
        in_specs=(P(None, "rows", "cols", None),) * 2 + (P(),) * 11,
        out_specs=P(None, "rows", "cols", None),
        check_vma=False,
    )
```
